1024 devices in a mesh: mom: 16 (over x, y_lo), en: 64 (over z, y_hi, core).
Axes of the slice: x: 8, y: 8 (y_hi: 4, y_lo: 2; y = y_hi * 2 + y_lo), z: 8, core: 2. Of those that a mesh axis runs over, the one named last changes fastest.
Arguments:
- retarded: bfloat16 [16, 64, 2, 768, 768], P('mom', 'en'), may hold values from -0.21875 to 0.21875
- injection: bfloat16 [16, 64, 2, 12, 768], P('mom', 'en'), may hold values from -6 to 6
- neighbours: int32 [64, 4], replicated, may hold values from 0 to 63, as said below
- bond_count: int32 [64], P('en'), may hold values from 1 to 4, as said below
- bond_mode: int32 [64, 4], P('en'), may hold values from 0 to 5
- mode_shift: int32 [6], replicated, may hold values from 1 to 8
- occupation: float32 [16, 6], replicated, may hold values from 0.1 to 4
- coupling: float32 [64, 4, 12, 12], P('en'), may hold values from -1.2 to 1.2
Outputs:
- scattering: float32 [16, 64, 64, 4, 144], P('mom', 'en')
The draws below stay inside these ranges and needn't reach their ends.
Inputs may be any that keep to these rules, and one draw needn't show every extreme that they name: `neighbours`: each row lists 4 different atoms, none equal to the row's own atom; only the first bond_count entries of a row are bonds. `bond_count`: some atom has 4 bonds.
All inputs are finite; a program needn't handle non-finite values.
Results may differ from the reference program's by a relative error of at most 0.0049.
Values may be sent and summed in bfloat16 or wider, within the bound.
No kernel may reach another device: no remote copies, remote signals or barrier semaphores. Data moves between devices by JAX's collectives and lax.ppermute only.
A program may use at most 32 MiB of HBM per device.

```python
import math
import jax
import jax.numpy as jnp
from jax import lax

NO = 12
ATOMS = 64
NB = 4
NMODES = 6
ORB = 768
ENERGIES = 64
MOMENTA = 16
SMAX = 8


def draw_neighbours(key, part):
    scores = jax.random.randint(key, (ATOMS, ATOMS), 0, 2 ** 20) * ATOMS + jnp.arange(ATOMS, dtype=jnp.int32)[None, :]
    scores = jnp.where(jnp.eye(ATOMS, dtype=bool), 2 ** 30, scores)
    ranked = jnp.argsort(scores, axis=1, stable=True)
    return ranked[:, :NB].astype(jnp.int32)


def draw_bond_count(key, part):
    first_key, second_key = jax.random.split(jax.random.fold_in(key, 7))
    counted = jax.random.randint(first_key, (ATOMS,), 1, NB + 1)
    chosen = jax.random.randint(second_key, (), 0, ATOMS)
    return counted.at[chosen].set(NB).astype(jnp.int32)


def plant(values, own_key, smallest, top_value):
    spot = [jax.random.randint(jax.random.fold_in(own_key, axis), (), 0, length) for axis, length in enumerate(values.shape)]
    widest = values.shape.index(max(values.shape))
    neighbour = spot[:widest] + [(spot[widest] + 1) % values.shape[widest]] + spot[widest + 1:]
    return values.at[tuple(spot)].set(smallest).at[tuple(neighbour)].set(top_value)


def block_levels(stream_key, extent, cuts, low, largest):
    level, own = 1.0, jax.random.fold_in(stream_key, 6)
    for position, blocks in cuts:
        steps = jnp.exp(jax.random.uniform(jax.random.fold_in(own, position), (blocks,), jnp.float32, low / len(cuts), largest / len(cuts)))
        level = level * jnp.repeat(steps, extent[position] // blocks).reshape([-1 if axis == position else 1 for axis in range(len(extent))])
    return level


def bell_draw(key, dims, width, reach, cuts=(), kind=jnp.bfloat16):
    loudness = block_levels(key, dims, cuts, -0.22, 0.18) if cuts else 1.0
    values = jax.random.normal(key, dims, jnp.float32) * width * loudness
    return jnp.minimum(jnp.maximum(values, -reach), reach).astype(kind)


def setup_inputs(seed: int = 0) -> dict:
    streams_of = jax.random.split(jax.random.key(seed), 9)
    return {
        "retarded": bell_draw(streams_of[0], (MOMENTA, ENERGIES, 2, ORB, ORB), ORB ** -0.5, 0.21875, ((0, 16), (1, 64))),
        "injection": bell_draw(streams_of[1], (MOMENTA, ENERGIES, 2, NO, ORB), 1.0, 6.0, ((0, 16), (1, 64))),
        "neighbours": draw_neighbours(jax.random.fold_in(streams_of[8], 71), 0),
        "bond_count": draw_bond_count(jax.random.fold_in(streams_of[8], 71), 0),
        "bond_mode": plant(jax.random.randint(streams_of[4], (ATOMS, NB), 0, NMODES), jax.random.fold_in(streams_of[4], 1), 0, NMODES - 1).astype(jnp.int32),
        "mode_shift": plant(jax.random.randint(streams_of[5], (NMODES,), 1, SMAX + 1), jax.random.fold_in(streams_of[5], 1), 1, SMAX).astype(jnp.int32),
        "occupation": jnp.clip(jnp.exp(jax.random.uniform(streams_of[6], (MOMENTA, NMODES), jnp.float32, math.log(0.1), math.log(4.0))), 0.1, 4.0),
        "coupling": bell_draw(streams_of[7], (ATOMS, NB, NO, NO), 0.2, 1.2, ((0, 64),), jnp.float32),
    }


def keldysh(retarded, injection):
    order = retarded.shape[1]
    orbital = injection.shape[1]
    atom_count = order // orbital
    real_part = retarded[0].astype(jnp.float32)
    imag_part = retarded[1].astype(jnp.float32)
    s_real = injection[0].astype(jnp.float32).reshape(orbital, atom_count, orbital)
    s_imag = injection[1].astype(jnp.float32).reshape(orbital, atom_count, orbital)
    real_cols = real_part.reshape(order, atom_count, orbital)
    imag_cols = imag_part.reshape(order, atom_count, orbital)

    def right_product(former, latter):
        return jnp.einsum("rbi,ibk->rbk", former, latter)

    left_real = (right_product(real_cols, s_real) - right_product(imag_cols, s_imag)).astype(jnp.bfloat16)
    left_imag = (right_product(real_cols, s_imag) + right_product(imag_cols, s_real)).astype(jnp.bfloat16)
    left_real = lax.optimization_barrier(left_real).astype(jnp.float32).reshape(atom_count, orbital, order)
    left_imag = lax.optimization_barrier(left_imag).astype(jnp.float32).reshape(atom_count, orbital, order)
    real_rows = real_part.reshape(atom_count, orbital, order)
    imag_rows = imag_part.reshape(atom_count, orbital, order)

    def row_product(former, latter):
        return jnp.einsum("bic,bkc->bik", former, latter)

    lesser_real = row_product(left_real, real_rows) + row_product(left_imag, imag_rows)
    lesser_imag = row_product(left_imag, real_rows) - row_product(left_real, imag_rows)
    diag_real = jnp.moveaxis(jnp.diagonal(real_part.reshape(atom_count, orbital, atom_count, orbital), axis1=0, axis2=2), -1, 0)
    diag_imag = jnp.moveaxis(jnp.diagonal(imag_part.reshape(atom_count, orbital, atom_count, orbital), axis1=0, axis2=2), -1, 0)
    greater_real = lesser_real + diag_real - jnp.swapaxes(diag_real, 1, 2)
    greater_imag = lesser_imag + diag_imag + jnp.swapaxes(diag_imag, 1, 2)
    stacked = jnp.stack([lesser_real, lesser_imag, greater_real, greater_imag], axis=1)
    return stacked.reshape(atom_count, 4 * orbital * orbital).astype(jnp.bfloat16)


def one_energy(inputs):
    return keldysh(inputs[0], inputs[1])


def reference(retarded, injection, neighbours, bond_count, bond_mode, mode_shift, occupation, coupling):
    momenta = retarded.shape[0]
    energies = retarded.shape[1]
    atom_count = neighbours.shape[0]
    bond_slots = neighbours.shape[1]
    orbital = coupling.shape[2]
    entries = orbital * orbital
    n_modes = mode_shift.shape[0]
    flat_ret = retarded.reshape((momenta * energies,) + retarded.shape[2:])
    flat_inj = injection.reshape((momenta * energies,) + injection.shape[2:])
    blocks = lax.map(one_energy, (flat_ret, flat_inj))
    blocks = blocks.reshape(momenta, energies, atom_count, 4, entries)
    stacks = blocks[:, :, neighbours]
    kron_pair = (coupling[:, :, :, None, :, None] * coupling[:, :, None, :, None, :]).reshape(atom_count, bond_slots, entries, entries)
    kron_pair = lax.optimization_barrier(kron_pair.astype(jnp.bfloat16)).astype(jnp.float32)
    mode_pick = bond_mode[:, :, None] == jnp.arange(n_modes, dtype=jnp.int32)[None, None, :]
    shift_bond = jnp.sum(jnp.where(mode_pick, mode_shift[None, None, :], 0), axis=-1).astype(jnp.int32)
    energy_index = jnp.arange(energies, dtype=jnp.int32)
    target_e = energy_index[None, None, :, None]
    source_e = energy_index[None, None, None, :]
    lower_map = (source_e == target_e - shift_bond[:, :, None, None]).astype(jnp.float32)
    upper_map = (source_e == target_e + shift_bond[:, :, None, None]).astype(jnp.float32)
    bond_live = (jnp.arange(bond_slots, dtype=jnp.int32)[None, :] < bond_count[:, None]).astype(jnp.float32)
    greater = jnp.array([0.0, 0.0, 1.0, 1.0], dtype=jnp.float32)
    targets = jnp.arange(momenta, dtype=jnp.int32)

    def per_source(running, inputs):
        source_stack, source = inputs
        imaged = jnp.einsum("amij,eamcj->ameci", kron_pair, source_stack.astype(jnp.float32))
        lower = jnp.einsum("amef,amfcx->amecx", lower_map, imaged, precision=lax.Precision.HIGHEST)
        upper = jnp.einsum("amef,amfcx->amecx", upper_map, imaged, precision=lax.Precision.HIGHEST)
        transfer = ((targets - source) % momenta).astype(jnp.int32)
        occupied_rows = occupation[transfer]
        occupied = jnp.sum(jnp.where(mode_pick[None], occupied_rows[:, None, None, :], 0.0), axis=-1)
        weight_low = bond_live[None, :, :, None] * (occupied[..., None] + greater)
        weight_high = bond_live[None, :, :, None] * (occupied[..., None] + 1.0 - greater)
        running = running + jnp.einsum("tamc,amecx->taecx", weight_low, lower, precision=lax.Precision.HIGHEST)
        running = running + jnp.einsum("tamc,amecx->taecx", weight_high, upper, precision=lax.Precision.HIGHEST)
        return running, None

    empty_sum = jnp.zeros((momenta, atom_count, energies, 4, entries), jnp.float32)
    running, unused = lax.scan(per_source, empty_sum, (stacks, jnp.arange(momenta, dtype=jnp.int32)))
    return running / momenta
```

```python
import functools

import jax
import jax.numpy as jnp
from jax import lax
from jax.experimental import pallas as pl
from jax.experimental.pallas import tpu as pltpu
from jax.sharding import PartitionSpec as P

F32, BF16, I32 = jnp.float32, jnp.bfloat16, jnp.int32
NO, NX, ATOMS, ROWS, ORD = 12, 144, 64, 256, 768
HALF, SUB, WIN = 384, 192, 256


def iota(shape, dim):
    return lax.broadcasted_iota(I32, shape, dim)


def one(mask):
    return jnp.where(mask, 1.0, 0.0).astype(BF16)


def dot(a, b):
    return lax.dot_general(a, b, (((1,), (0,)), ((), ())), preferred_element_type=F32)


def dot_t(a, b):
    return lax.dot_general(a, b, (((1,), (1,)), ((), ())), preferred_element_type=F32)


def pick_lanes(parts):
    lane = iota((ROWS, 128), 1)
    tiles = [parts[0][:, :128]]
    for t in range(1, 4):
        tiles.append(jnp.where(lane < 16 * t, parts[t - 1][:, 128:], parts[t][:, :128]))
    tiles.append(parts[3][:, 128:])
    return tiles


def blocks_kernel(nb_ref, g_ref, s_ref, out_ref, z_ref):
    spread = one(iota((HALF, NO), 0) % NO == iota((HALF, NO), 1))
    same = iota((HALF, ORD), 0) // NO == (iota((HALF, ORD), 1) % HALF) // NO
    left, right_r, right_i = [], [], []
    for t in range(2):
        cols = slice(HALF * t, HALF * (t + 1))
        g_r, g_i = g_ref[0, :, cols], g_ref[1, :, cols]
        s_r, s_i = s_ref[0, :, cols], s_ref[1, :, cols]
        upper = dot(spread, jnp.concatenate([s_r, s_i], axis=1))
        lower = dot(spread, jnp.concatenate([-s_i, s_r], axis=1))
        factor = jnp.concatenate(
            [jnp.where(same, upper, 0.0).astype(BF16), jnp.where(same, lower, 0.0).astype(BF16)], axis=0
        )
        both = jnp.concatenate([g_r, g_i], axis=1)
        left.append(dot(both, factor).astype(BF16))
        right_r.append(both)
        right_i.append(jnp.concatenate([-g_i, g_r], axis=1))
    left = jnp.concatenate(left, axis=1)
    right_r = jnp.concatenate(right_r, axis=1)
    right_i = jnp.concatenate(right_i, axis=1)
    own = iota((SUB, NX), 1) // NO == iota((SUB, NX), 0) % NO
    for h in range(4):
        rows = slice(SUB * h, SUB * (h + 1))
        odd = h % 2
        base = HALF * (h // 2) + 128 * odd
        window = slice(base, base + WIN)
        block = slice(HALF * (h // 2), HALF * (h // 2 + 1))
        mine = left[rows]
        turn = one(iota((SUB, HALF), 1) == iota((SUB, HALF), 0) + SUB * odd)
        diagonal = (iota((SUB, WIN), 0) + SUB * odd) // NO == (iota((SUB, WIN), 1) + 128 * odd) // NO
        fold = one((iota((WIN, NX), 0) + 128 * odd) % NO == iota((WIN, NX), 1) % NO)
        for part, right, sign in ((0, right_r, -1.0), (1, right_i, 1.0)):
            lesser = dot_t(mine, right[window])
            plain = g_ref[part, rows, window].astype(F32)
            turned = dot_t(turn, g_ref[part, window, block])
            greater = lesser + (plain + sign * turned)
            for c, value in ((part, lesser), (2 + part, greater)):
                folded = dot(jnp.where(diagonal, value, 0.0).astype(BF16), fold)
                z_ref[c, rows, :] = jnp.where(own, folded, 0.0).astype(BF16)
    gather = one(iota((ATOMS, ORD), 1) // NO == iota((ATOMS, ORD), 0))
    blocks = jnp.concatenate([dot(gather, z_ref[c]).astype(BF16) for c in range(4)], axis=0)
    tiled = dot(blocks, one(iota((NX, 640), 1) % NX == iota((NX, 640), 0))).astype(BF16)
    column = iota((ROWS, ROWS), 1)
    row = iota((ROWS, ROWS), 0)
    parts = []
    for m in range(4):
        wanted = (row & 3) * ATOMS + nb_ref[:, m : m + 1]
        parts.append(dot(one(column == wanted), tiled[:, 128 * m : 128 * m + WIN]))
    tiles = pick_lanes(parts)
    packed = jnp.concatenate(tiles, axis=1)[:, : 4 * NX]
    out_ref[...] = packed.reshape(ATOMS, 4, 4 * NX).astype(BF16)


def image_kernel(shift_ref, live_ref, c_ref, p_ref, out_ref):
    rows, lanes = iota((4 * NX, 4 * NX), 0), iota((4 * NX, 4 * NX), 1)
    coupling = c_ref[...]
    factors = []
    for outer in (True, False):
        lane = iota((NO, 4 * NX), 1)
        wide = (lane % NX) // NO if outer else lane % NO
        spread = jnp.where(iota((NO, 4 * NX), 0) == wide, 1.0, 0.0)
        wide = lax.dot_general(
            coupling, spread, (((1,), (0,)), ((), ())), precision=lax.Precision.HIGHEST, preferred_element_type=F32
        )
        high = wide.astype(BF16)
        rest = wide - high.astype(F32)
        middle = rest.astype(BF16)
        low = (rest - middle.astype(F32)).astype(BF16)
        stacked = jnp.concatenate([high, middle, low], axis=0)
        row = iota((4 * NX, 3 * 48), 0)
        source = (row // NX) * NO + ((row % NX) // NO if outer else row % NO)
        factors.append(dot(one(iota((4 * NX, 3 * 48), 1) % 48 == source), stacked))
    kron = jnp.where(rows // NX == lanes // NX, factors[0] * factors[1], 0.0).astype(BF16)
    pieces = p_ref[...].astype(F32).reshape(ROWS, 4 * NX).astype(BF16)
    imaged = dot(pieces, kron).astype(BF16)
    imaged = jnp.concatenate([imaged, jnp.zeros((ROWS, 64), BF16)], axis=1)
    row, column = iota((ROWS, ROWS), 0), iota((ROWS, ROWS), 1)
    gap = column - row
    is_greater = (row & 2) > 0
    pairs, totals = [], []
    for m in range(4):
        step = 4 * shift_ref[m]
        window = imaged[:, 128 * m : 128 * m + WIN]
        lower, upper = gap == -step, gap == step
        weight = live_ref[m].astype(F32)
        both = jnp.where(lower | upper, weight, 0.0).astype(BF16)
        single = jnp.where(jnp.where(is_greater, -gap, gap) == step, weight, 0.0).astype(BF16)
        pairs.append(dot(both, window))
        totals.append(dot(single, window))
    tiles = pick_lanes(pairs)
    sums = jnp.concatenate(pick_lanes(totals), axis=1).astype(BF16)
    lane, target = iota((640, WIN), 0), iota((640, WIN), 1) - 64
    fold = one((lane < 4 * NX) & (target >= 0) & (target < NX) & (lane % NX == target))
    total = dot(sums, fold)
    last = jnp.where(iota((ROWS, 128), 1) < 64, tiles[4], total[:, :128])
    for t, tile in enumerate([*tiles[:4], last, total[:, 128:]]):
        out_ref[:, 128 * t : 128 * (t + 1)] = tile.astype(BF16)


def momentum_kernel(n_ref, v_ref, out_ref):
    row, lane = iota((16, ROWS), 0), iota((16, ROWS), 1)
    transfer = (row - lane // 16) & 15
    spread = one(iota((ROWS, 16), 0) // 16 == iota((ROWS, 16), 1))
    same = (iota((ROWS, ROWS), 0) & 15) == (iota((ROWS, ROWS), 1) & 15)
    acc = jnp.zeros((ROWS, NX), F32)
    for m in range(5):
        window = v_ref[:, 128 * m : 128 * m + WIN]
        move = one(iota((WIN, NX), 0) == iota((WIN, NX), 1) + 16 * m)
        pieces = dot(window, move).astype(BF16)
        if m == 4:
            acc += dot(jnp.where(same, 1.0 / 16, 0.0).astype(BF16), pieces)
            continue
        weights = jnp.zeros((16, ROWS), F32)
        for q in range(16):
            weights = jnp.where(transfer == q, n_ref[m, q] * (1.0 / 16), weights)
        high = weights.astype(BF16)
        low = (weights - high.astype(F32)).astype(BF16)
        for part in (high, low):
            acc += dot(jnp.where(same, dot(spread, part), 0.0).astype(BF16), pieces)
    out_ref[...] = acc.astype(BF16)


VMEM = pl.BlockSpec(memory_space=pltpu.VMEM)
SMEM = pl.BlockSpec(memory_space=pltpu.SMEM)


def call(kernel, out, specs, scratch=()):
    return pl.pallas_call(
        kernel,
        out_shape=jax.ShapeDtypeStruct(out, BF16),
        in_specs=specs,
        out_specs=VMEM,
        scratch_shapes=scratch,
        compiler_params=pltpu.CompilerParams(vmem_limit_bytes=48 << 20),
    )


def blocks_of(neighbours, retarded, injection):
    rows = jnp.repeat(neighbours, 4, axis=0)
    f = call(blocks_kernel, (ATOMS, 4, 4 * NX), [VMEM, VMEM, VMEM], [pltpu.VMEM((4, ORD, NX), BF16)])
    return f(rows, retarded, injection)


def image_of(shift, live, coupling, pieces):
    turned = jnp.swapaxes(coupling, 1, 2).reshape(4 * NO, NO)
    return call(image_kernel, (ROWS, ORD), [SMEM, SMEM, VMEM, VMEM])(shift, live, turned, pieces)


def convolved(occupied, pieces):
    return call(momentum_kernel, (ROWS, NX), [SMEM, VMEM])(occupied, pieces)


def exchange(x, axis):
    return lax.all_to_all(x, axis, split_axis=0, concat_axis=0, tiled=True)


def per_device(retarded, injection, neighbours, bond_count, bond_mode, mode_shift, occupation, coupling):
    shift = mode_shift[bond_mode[0]]
    live = (jnp.arange(4, dtype=I32) < bond_count[0]).astype(I32)
    occupied = occupation.T[bond_mode[0]]
    sent = blocks_of(neighbours, retarded[0, 0], injection[0, 0])
    pieces = exchange(sent, "en")
    imaged = image_of(shift, live, coupling[0], pieces)
    spread = exchange(imaged.reshape(16, 16, ORD), "mom")
    scattered = convolved(occupied, spread.reshape(ROWS, ORD))
    back = exchange(scattered.reshape(16, 16, NX), "mom")
    return back.reshape(1, 1, ATOMS, 4, NX).astype(F32)


def solution(mesh):
    en = P("en")
    in_specs = (
        P("mom", "en", None, None, None),
        P("mom", "en", None, None, None),
        P(),
        en,
        P("en", None),
        P(),
        P(),
        P("en", None, None, None),
    )
    return jax.shard_map(
        per_device,
        mesh=mesh,
        in_specs=in_specs,
        out_specs=P("mom", "en", None, None, None),
        check_vma=False,
    )
```

```python
import functools

import jax
import jax.numpy as jnp
from jax import lax
from jax.experimental import pallas as pl
from jax.experimental.pallas import tpu as pltpu
from jax.sharding import PartitionSpec as P

F32, BF16, I32 = jnp.float32, jnp.bfloat16, jnp.int32
NO, NX, ATOMS, ROWS, ORD = 12, 144, 64, 256, 768
HALF, SUB, WIN = 384, 192, 256


def iota(shape, dim):
    return lax.broadcasted_iota(I32, shape, dim)


def one(mask):
    return jnp.where(mask, 1.0, 0.0).astype(BF16)


def dot(a, b):
    return lax.dot_general(a, b, (((1,), (0,)), ((), ())), preferred_element_type=F32)


def dot_t(a, b):
    return lax.dot_general(a, b, (((1,), (1,)), ((), ())), preferred_element_type=F32)


def pick_lanes(parts):
    lane = iota((ROWS, 128), 1)
    tiles = [parts[0][:, :128]]
    for t in range(1, 4):
        tiles.append(jnp.where(lane < 16 * t, parts[t - 1][:, 128:], parts[t][:, :128]))
    tiles.append(parts[3][:, 128:])
    return tiles


def blocks_kernel(nb_hbm, s_hbm, g_hbm, out_ref, nb_ref, s_ref, g_ref, left_ref, z_ref, sems):
    small = [pltpu.make_async_copy(s_hbm, s_ref, sems.at[4]), pltpu.make_async_copy(nb_hbm, nb_ref, sems.at[5])]
    for copy in small:
        copy.start()
    copies = []
    for t in range(2):
        for part in range(2):
            rows = pl.ds(HALF * t, HALF)
            copies.append(
                pltpu.make_async_copy(g_hbm.at[part, rows, :], g_ref.at[part, rows, :], sems.at[2 * t + part])
            )
    for copy in copies:
        copy.start()
    for copy in small:
        copy.wait()
    spread = one((iota((128, NO), 0) + 8) % NO == iota((128, NO), 1))
    s_r = s_ref[:, 0, :].astype(F32)
    s_i = s_ref[:, 1, :].astype(F32)
    tall, wide = iota((128, 128), 0), iota((128, 128), 1)
    factors = []
    for t in range(6):
        cols = slice(128 * t, 128 * (t + 1))
        both = jnp.concatenate([s_r[:, cols], s_i[:, cols]], axis=1).astype(BF16)
        for shifts in ((0, 0), (1, -1)):
            near = jnp.where(tall < 64, 128 * (t + shifts[0]), 128 * (t + shifts[1])) + tall
            orbital = jnp.where(
                iota((128, NO), 0) < 64, 128 * (t + shifts[0]) + 240, 128 * (t + shifts[1]) + 240
            ) + iota((128, NO), 0)
            pick = one(orbital % NO == iota((128, NO), 1))
            rows = dot(pick, both)
            same = (near + 240) // NO == (128 * t + wide + 240) // NO
            real = jnp.where(same, rows[:, :128], 0.0)
            imag = jnp.where(same, rows[:, 128:], 0.0)
            upper = jnp.concatenate([real, imag], axis=1)
            lower = jnp.concatenate([-imag, real], axis=1)
            factors.append(jnp.concatenate([upper, lower], axis=0).astype(BF16))
    lane = iota((HALF, 128), 1)
    own = iota((4 * SUB, NX), 1) // NO == iota((4 * SUB, NX), 0) % NO
    for half in range(2):
        rows = slice(HALF * half, HALF * (half + 1))
        copies[2 * half].wait()
        copies[2 * half + 1].wait()
        tiles = [[g_ref[part, rows, 128 * t : 128 * (t + 1)] for part in range(2)] for t in range(6)]
        for t in range(6):
            low, high = tiles[max(t - 1, 0)], tiles[min(t + 1, 5)]
            beside = [jnp.where(lane < 64, high[part], low[part]) for part in range(2)]
            line = dot(jnp.concatenate(tiles[t], axis=1), factors[2 * t])
            line += dot(jnp.concatenate(beside, axis=1), factors[2 * t + 1])
            line = line.astype(BF16)
            left_ref[0, :, 256 * t : 256 * t + 256] = line
            left_ref[1, :, 256 * t : 256 * t + 128] = line[:, 128:]
            left_ref[1, :, 256 * t + 128 : 256 * t + 256] = -line[:, :128]
        right = jnp.concatenate([piece for tile in tiles for piece in tile], axis=1)
        for odd in range(2):
            mine = slice(SUB * odd, SUB * (odd + 1))
            window = slice(128 * odd, 128 * odd + WIN)
            stacked = jnp.concatenate([left_ref[0, mine, :], left_ref[1, mine, :]], axis=0)
            lesser = dot_t(stacked, right[window])
            turn = one(iota((SUB, WIN), 1) + 128 * odd == iota((SUB, WIN), 0) + SUB * odd)
            base = HALF * half
            square = slice(base + 128 * odd, base + 128 * odd + WIN)
            values = [lesser[:SUB], lesser[SUB:]]
            for part, sign in ((0, -1.0), (1, 1.0)):
                plain = g_ref[part, base + SUB * odd : base + SUB * (odd + 1), square].astype(F32)
                turned = dot_t(turn, g_ref[part, square, square])
                values.append(values[part] + (plain + sign * turned))
            diagonal = (iota((SUB, WIN), 0) + SUB * odd) // NO == (iota((SUB, WIN), 1) + 128 * odd) // NO
            fold = one((iota((WIN, NX), 0) + 128 * odd) % NO == iota((WIN, NX), 1) % NO)
            kept = jnp.concatenate([jnp.where(diagonal, v, 0.0).astype(BF16) for v in values], axis=0)
            folded = jnp.where(own, dot(kept, fold), 0.0).astype(BF16)
            for c in range(4):
                z_ref[c, base + SUB * odd : base + SUB * (odd + 1), :] = folded[SUB * c : SUB * (c + 1)]
    gather = one(iota((ATOMS, ORD), 1) // NO == iota((ATOMS, ORD), 0))
    blocks = jnp.concatenate([dot(gather, z_ref[c]).astype(BF16) for c in range(4)], axis=0)
    tiled = dot(blocks, one(iota((NX, 640), 1) % NX == iota((NX, 640), 0))).astype(BF16)
    column, row = iota((ROWS, ROWS), 1), iota((ROWS, ROWS), 0)
    owner = one(iota((ROWS, ATOMS), 0) // 4 == iota((ROWS, ATOMS), 1))
    atoms = dot_t(owner, nb_ref[...].astype(F32).astype(BF16)).astype(I32)
    parts = []
    for m in range(4):
        wanted = (row & 3) * ATOMS + atoms[:, m : m + 1]
        parts.append(dot(one(column == wanted), tiled[:, 128 * m : 128 * m + WIN]))
    packed = jnp.concatenate(pick_lanes(parts), axis=1)[:, : 4 * NX]
    out_ref[...] = packed.reshape(ATOMS, 4, 4 * NX).astype(BF16)


def prepare_kernel(mode_ref, n_ref, c_ref, kron_ref, weight_ref):
    rows, lanes = iota((4 * NX, 4 * NX), 0), iota((4 * NX, 4 * NX), 1)
    coupling = jnp.concatenate([c_ref[m].T for m in range(4)], axis=0)
    factors = []
    for outer in (True, False):
        lane = iota((NO, 4 * NX), 1)
        wide = (lane % NX) // NO if outer else lane % NO
        spread = jnp.where(iota((NO, 4 * NX), 0) == wide, 1.0, 0.0)
        wide = lax.dot_general(
            coupling, spread, (((1,), (0,)), ((), ())), precision=lax.Precision.HIGHEST, preferred_element_type=F32
        )
        high = wide.astype(BF16)
        rest = wide - high.astype(F32)
        middle = rest.astype(BF16)
        low = (rest - middle.astype(F32)).astype(BF16)
        stacked = jnp.concatenate([high, middle, low], axis=0)
        row = iota((4 * NX, 3 * 48), 0)
        source = (row // NX) * NO + ((row % NX) // NO if outer else row % NO)
        factors.append(dot(one(iota((4 * NX, 3 * 48), 1) % 48 == source), stacked))
    kron_ref[...] = jnp.where(rows // NX == lanes // NX, factors[0] * factors[1], 0.0).astype(BF16)
    row, lane = iota((16, ROWS), 0), iota((16, ROWS), 1)
    transfer = (row - lane // 16) & 15
    spread = one(iota((ROWS, 16), 0) // 16 == iota((ROWS, 16), 1))
    same = (iota((ROWS, ROWS), 0) & 15) == (iota((ROWS, ROWS), 1) & 15)
    for m in range(4):
        weights = jnp.zeros((16, ROWS), F32)
        for q in range(16):
            weights = jnp.where(transfer == q, n_ref[mode_ref[0, m], q] * (1.0 / 16), weights)
        high = weights.astype(BF16)
        low = (weights - high.astype(F32)).astype(BF16)
        for i, part in enumerate((high, low)):
            weight_ref[2 * m + i] = jnp.where(same, dot(spread, part), 0.0).astype(BF16)


def image_kernel(count_ref, mode_ref, shift_ref, kron_ref, p_ref, out_ref):
    pieces = p_ref[...].astype(F32).reshape(ROWS, 4 * NX).astype(BF16)
    imaged = dot(pieces, kron_ref[...]).astype(BF16)
    imaged = jnp.concatenate([imaged, jnp.zeros((ROWS, 64), BF16)], axis=1)
    row, column = iota((ROWS, ROWS), 0), iota((ROWS, ROWS), 1)
    gap = column - row
    facing = jnp.where((row & 2) > 0, -gap, gap)
    pairs, totals = [], []
    for m in range(4):
        step = jnp.where(m < count_ref[0], 4 * shift_ref[mode_ref[0, m]], 4 * ROWS)
        window = imaged[:, 128 * m : 128 * m + WIN]
        pairs.append(dot(one(jnp.abs(gap) == step), window))
        totals.append(dot(one(facing == step), window))
    tiles = pick_lanes(pairs)
    sums = jnp.concatenate(pick_lanes(totals), axis=1).astype(BF16)
    lane, target = iota((640, WIN), 0), iota((640, WIN), 1) - 64
    fold = one((lane < 4 * NX) & (target >= 0) & (target < NX) & (lane % NX == target))
    total = dot(sums, fold)
    last = jnp.where(iota((ROWS, 128), 1) < 64, tiles[4], total[:, :128])
    for t, tile in enumerate([*tiles[:4], last, total[:, 128:]]):
        out_ref[:, 128 * t : 128 * (t + 1)] = tile.astype(BF16)


def momentum_kernel(weight_ref, v_ref, out_ref):
    same = (iota((ROWS, ROWS), 0) & 15) == (iota((ROWS, ROWS), 1) & 15)
    acc = jnp.zeros((ROWS, NX), F32)
    for m in range(5):
        window = v_ref[:, 128 * m : 128 * m + WIN]
        move = one(iota((WIN, NX), 0) == iota((WIN, NX), 1) + 16 * m)
        pieces = dot(window, move).astype(BF16)
        if m == 4:
            acc += dot(jnp.where(same, 1.0 / 16, 0.0).astype(BF16), pieces)
        else:
            acc += dot(weight_ref[2 * m], pieces) + dot(weight_ref[2 * m + 1], pieces)
    out_ref[...] = acc.astype(BF16)


VMEM = pl.BlockSpec(memory_space=pltpu.VMEM)
SMEM = pl.BlockSpec(memory_space=pltpu.SMEM)
HBM = pl.BlockSpec(memory_space=pltpu.HBM)


def call(kernel, outs, specs, scratch=()):
    shapes = [jax.ShapeDtypeStruct(out, BF16) for out in outs]
    return pl.pallas_call(
        kernel,
        out_shape=shapes if len(outs) > 1 else shapes[0],
        in_specs=specs,
        out_specs=[VMEM] * len(outs) if len(outs) > 1 else VMEM,
        scratch_shapes=scratch,
        compiler_params=pltpu.CompilerParams(vmem_limit_bytes=48 << 20),
    )


def blocks_of(neighbours, retarded, injection):
    scratch = [
        pltpu.VMEM((4, ATOMS), I32),
        pltpu.VMEM((NO, 2, ORD), BF16),
        pltpu.VMEM((2, ORD, ORD), BF16),
        pltpu.VMEM((2, HALF, 2 * ORD), BF16),
        pltpu.VMEM((4, ORD, NX), BF16),
        pltpu.SemaphoreType.DMA((6,)),
    ]
    f = call(blocks_kernel, [(ATOMS, 4, 4 * NX)], [HBM, HBM, HBM], scratch)
    operands = (neighbours.T, jnp.swapaxes(injection, 0, 1), retarded)
    return f(*(pltpu.with_memory_space_constraint(x, pltpu.HBM) for x in operands))


def prepared(bond_mode, occupation, coupling):
    f = call(prepare_kernel, [(4 * NX, 4 * NX), (8, ROWS, ROWS)], [SMEM, SMEM, VMEM])
    return f(bond_mode, occupation.T, coupling)


def image_of(bond_count, bond_mode, mode_shift, kron, pieces):
    f = call(image_kernel, [(ROWS, ORD)], [SMEM, SMEM, SMEM, VMEM, VMEM])
    return f(bond_count, bond_mode, mode_shift, kron, pieces)


def convolved(weights, pieces):
    return call(momentum_kernel, [(ROWS, NX)], [VMEM, VMEM])(weights, pieces)


def exchange(x, axis):
    return lax.all_to_all(x, axis, split_axis=0, concat_axis=0, tiled=True)


def per_device(retarded, injection, neighbours, bond_count, bond_mode, mode_shift, occupation, coupling):
    sent = blocks_of(neighbours, retarded[0, 0], injection[0, 0])
    kron, weights = prepared(bond_mode, occupation, coupling[0])
    pieces = exchange(sent, "en")
    imaged = image_of(bond_count, bond_mode, mode_shift, kron, pieces)
    spread = exchange(imaged.reshape(16, 16, ORD), "mom")
    scattered = convolved(weights, spread.reshape(ROWS, ORD))
    back = exchange(scattered.reshape(16, 16, NX), "mom")
    return back.reshape(1, 1, ATOMS, 4, NX).astype(F32)


def solution(mesh):
    en = P("en")
    in_specs = (
        P("mom", "en", None, None, None),
        P("mom", "en", None, None, None),
        P(),
        en,
        P("en", None),
        P(),
        P(),
        P("en", None, None, None),
    )
    return jax.shard_map(
        per_device,
        mesh=mesh,
        in_specs=in_specs,
        out_specs=P("mom", "en", None, None, None),
        check_vma=False,
    )
```

```python
import functools

import jax
import jax.numpy as jnp
from jax import lax
from jax.experimental import pallas as pl
from jax.experimental.pallas import tpu as pltpu
from jax.sharding import PartitionSpec as P

F32, BF16, I32 = jnp.float32, jnp.bfloat16, jnp.int32
NO, NX, ATOMS, ROWS, ORD = 12, 144, 64, 256, 768
HALF, SUB, WIN = 384, 192, 256


def iota(shape, dim):
    return lax.broadcasted_iota(I32, shape, dim)


def one(mask):
    return jnp.where(mask, 1.0, 0.0).astype(BF16)


def dot(a, b):
    return lax.dot_general(a, b, (((1,), (0,)), ((), ())), preferred_element_type=F32)


def dot_t(a, b):
    return lax.dot_general(a, b, (((1,), (1,)), ((), ())), preferred_element_type=F32)


def pick_lanes(parts):
    lane = iota((ROWS, 128), 1)
    tiles = [parts[0][:, :128]]
    for t in range(1, 4):
        tiles.append(jnp.where(lane < 16 * t, parts[t - 1][:, 128:], parts[t][:, :128]))
    tiles.append(parts[3][:, 128:])
    return tiles


def atom_of(index):
    return (index * 5462) >> 16


def orbital_of(index):
    return index - NO * atom_of(index)


def blocks_kernel(nb_hbm, s_hbm, g_hbm, out_ref, nb_ref, s_ref, g_ref, left_ref, z_ref, sems):
    small = [pltpu.make_async_copy(s_hbm, s_ref, sems.at[4]), pltpu.make_async_copy(nb_hbm, nb_ref, sems.at[5])]
    copies = []
    for t in range(2):
        for part in range(2):
            rows = pl.ds(HALF * t, HALF)
            copies.append(
                pltpu.make_async_copy(g_hbm.at[part, rows, :], g_ref.at[part, rows, :], sems.at[2 * t + part])
            )
    for copy in small + copies:
        copy.start()
    for copy in small:
        copy.wait()
    s_r = s_ref[:, 0, :].astype(F32)
    s_i = s_ref[:, 1, :].astype(F32)
    tall, thin = iota((128, 128), 0), iota((128, NO), 0)
    wide, slot = iota((1, 128), 1), iota((1, NO), 1)
    factors = []
    for t in range(6):
        cols = slice(128 * t, 128 * (t + 1))
        upper = jnp.concatenate([s_r[:, cols], s_i[:, cols]], axis=1).astype(BF16)
        lower = jnp.concatenate([-s_i[:, cols], s_r[:, cols]], axis=1).astype(BF16)
        mine = atom_of(wide + (128 * t + 240))
        for kind in range(2):
            if kind:
                near = tall + jnp.where(tall < 64, 128 * (t + 1) + 240, 128 * (t - 1) + 240)
                pick = thin + jnp.where(thin < 64, 128 * (t + 1) + 240, 128 * (t - 1) + 240)
            else:
                near, pick = tall + (128 * t + 240), thin + (128 * t + 240)
            spread = one(orbital_of(pick) == slot)
            same = atom_of(near) == mine
            same = jnp.concatenate([same, same], axis=1)
            halves = [jnp.where(same, dot(spread, x), 0.0).astype(BF16) for x in (upper, lower)]
            factors.append(jnp.concatenate(halves, axis=0))
    lane = iota((HALF, 128), 1)
    for half in range(2):
        rows = slice(HALF * half, HALF * (half + 1))
        copies[2 * half].wait()
        copies[2 * half + 1].wait()
        tiles = [[g_ref[part, rows, 128 * t : 128 * (t + 1)] for part in range(2)] for t in range(6)]
        for t in range(6):
            low, high = tiles[max(t - 1, 0)], tiles[min(t + 1, 5)]
            beside = [jnp.where(lane < 64, high[part], low[part]) for part in range(2)]
            line = dot(jnp.concatenate(tiles[t], axis=1), factors[2 * t])
            line += dot(jnp.concatenate(beside, axis=1), factors[2 * t + 1])
            line = line.astype(BF16)
            left_ref[0, rows, 256 * t : 256 * t + 256] = line
            left_ref[1, rows, 256 * t : 256 * t + 128] = line[:, 128:]
            left_ref[1, rows, 256 * t + 128 : 256 * t + 256] = -line[:, :128]
    own = atom_of(iota((1, NX), 1)) == orbital_of(iota((SUB, NX), 0))

    def products(half, odd):
        mine = slice(HALF * half + SUB * odd, HALF * half + SUB * (odd + 1))
        window = slice(HALF * half + 128 * odd, HALF * half + 128 * odd + WIN)
        stacked = jnp.concatenate([left_ref[0, mine, :], left_ref[1, mine, :]], axis=0)
        cols = [slice(128 * t, 128 * (t + 1)) for t in range(6)]
        right = jnp.concatenate([g_ref[part, window, col] for col in cols for part in range(2)], axis=1)
        return dot_t(stacked, right)

    def finish(half, odd, lesser):
        base = HALF * half
        square = slice(base + 128 * odd, base + 128 * odd + WIN)
        inner = slice(64 * odd, 64 * odd + SUB)
        shift = []
        for part, sign in ((0, -1.0), (1, 1.0)):
            plain = g_ref[part, square, square].astype(F32)
            shift.append(plain[inner] + sign * plain.T[inner])
        row, col = iota((SUB, WIN), 0) + SUB * odd, iota((1, WIN), 1) + 128 * odd
        diagonal = atom_of(row) == atom_of(col)
        fold = one(orbital_of(iota((WIN, NX), 0) + 128 * odd) == orbital_of(iota((1, NX), 1)))
        values = [lesser[:SUB], lesser[SUB:], jnp.where(row > col, shift[0], shift[1])]
        for c, value in enumerate(values):
            folded = dot(jnp.where(diagonal, value, 0.0).astype(BF16), fold)
            z_ref[c, base + SUB * odd : base + SUB * (odd + 1), :] = jnp.where(own, folded, 0.0).astype(BF16)

    todo = [(0, 0), (0, 1), (1, 0), (1, 1)]
    ahead = products(*todo[0])
    for w in range(4):
        lesser = ahead
        if w < 3:
            ahead = products(*todo[w + 1])
        finish(*todo[w], lesser)
    gather = one(atom_of(iota((ATOMS, ORD), 1)) == iota((ATOMS, ORD), 0))
    blocks = jnp.concatenate([dot(gather, z_ref[c]) for c in range(3)], axis=1).astype(BF16)
    owner = one(iota((ROWS, ATOMS), 0) >> 2 == iota((ROWS, ATOMS), 1))
    atoms = dot_t(owner, nb_ref[...].astype(F32).astype(BF16)).astype(I32)
    bond = iota((ROWS, 1), 0) & 3
    wanted = atoms[:, 0:1]
    for m in range(1, 4):
        wanted = jnp.where(bond == m, atoms[:, m : m + 1], wanted)
    sent = dot(one(iota((ROWS, ATOMS), 1) == wanted), blocks)
    out_ref[...] = sent.reshape(ATOMS, 4, 3 * NX).astype(BF16)


def prepare_kernel(count_ref, mode_ref, shift_ref, n_ref, c_ref, kron_ref, weight_ref, turn_ref, move_ref, step_ref, fold_ref):
    factors = []
    for outer in (True, False):
        pieces = []
        for m in range(4):
            x = iota((NO, WIN), 1) - 16 * m
            inside = (x >= 0) & (x < NX)
            wide = (atom_of if outer else orbital_of)(jnp.maximum(x, 0))
            spread = jnp.where(inside & (iota((NO, WIN), 0) == wide), 1.0, 0.0)
            pieces.append(
                lax.dot_general(
                    c_ref[m].T, spread, (((1,), (0,)), ((), ())), precision=lax.Precision.HIGHEST, preferred_element_type=F32
                )
            )
        wide = jnp.concatenate(pieces, axis=0)
        high = wide.astype(BF16)
        rest = wide - high.astype(F32)
        middle = rest.astype(BF16)
        low = (rest - middle.astype(F32)).astype(BF16)
        stacked = jnp.concatenate([high, middle, low], axis=0)
        row = iota((4 * NX, 3 * 48), 0)
        j = atom_of(row)
        source = j if outer else NO * (atom_of(j)) + row - NO * j
        factors.append(dot(one(orbital_of(iota((1, 3 * 48), 1)) + NO * (atom_of(iota((1, 3 * 48), 1)) & 3) == source), stacked))
    kron_ref[...] = (factors[0] * factors[1]).astype(BF16)
    row, lane = iota((16, ROWS), 0), iota((16, ROWS), 1)
    transfer = (row - lane // 16) & 15
    spread = one(iota((ROWS, 16), 0) // 16 == iota((ROWS, 16), 1))
    same = (iota((ROWS, ROWS), 0) & 15) == (iota((ROWS, ROWS), 1) & 15)
    for m in range(4):
        weights = jnp.zeros((16, ROWS), F32)
        for q in range(16):
            weights = jnp.where(transfer == q, n_ref[mode_ref[0, m], q] * (1.0 / 16), weights)
        high = weights.astype(BF16)
        low = (weights - high.astype(F32)).astype(BF16)
        for i, part in enumerate((high, low)):
            weight_ref[2 * m + i] = jnp.where(same, dot(spread, part), 0.0).astype(BF16)
    row, column = iota((ROWS, ROWS), 0), iota((ROWS, ROWS), 1)
    turn_ref[...] = one(column == ((row & 63) << 2) + (row >> 6))
    x = iota((1, NX), 1)
    upper = orbital_of(x)
    swapped = NO * upper + atom_of(x)
    below = upper < atom_of(x)
    lane = iota((WIN, NX), 0)
    for c in range(2):
        move_ref[c] = one(lane == x + 16 * c)
    kept = jnp.where(lane - 32 == x, 1.0, 0.0)
    turned = jnp.where(lane - 32 == swapped, 1.0, 0.0)
    move_ref[2] = jnp.where(below, kept, jnp.where(x == swapped, 0.0, -turned)).astype(BF16)
    move_ref[3] = jnp.where(below, turned, kept).astype(BF16)
    part = (row & 3) - (column >> 6)
    gap = (column & 63) - (row >> 2)
    gap = jnp.where((part == 0) | (part == 2), gap, 8 * ROWS)
    facing = jnp.where((row & 2) > 0, -gap, gap)
    gap = jnp.abs(gap)
    for m in range(4):
        step = jnp.where(m < count_ref[0], shift_ref[mode_ref[0, m]], 4 * ROWS)
        step_ref[m, :ROWS, :] = one(gap == step)
        step_ref[m, ROWS:, :] = one(facing == step)
    lane, target = iota((640, WIN), 0), iota((1, WIN), 1) - 64
    source = lane
    for m in range(3):
        source = jnp.where(source >= NX, source - NX, source)
    fold_ref[...] = one((source == target) & (target < NX))


def image_kernel(kron_ref, turn_ref, move_ref, step_ref, fold_ref, p_ref, out_ref):
    pieces = p_ref[...].astype(F32).reshape(ROWS, 3 * NX).astype(BF16)
    pieces = dot(turn_ref[...], pieces).astype(BF16)
    parts = [dot(pieces[:, 128 * c : 128 * c + WIN], move_ref[c]).astype(BF16) for c in range(2)]
    parts += [dot(pieces[:, WIN:], move_ref[c, :176, :]).astype(BF16) for c in (2, 3)]
    windows = []
    for m in range(4):
        bond = jnp.concatenate([value[ATOMS * m : ATOMS * (m + 1)] for value in parts], axis=0)
        windows.append(dot(bond, kron_ref[NX * m : NX * (m + 1), :]).astype(BF16))
    shifted = [dot(step_ref[m], windows[m]) for m in range(4)]
    tiles = pick_lanes([both[:ROWS] for both in shifted])
    sums = jnp.concatenate(pick_lanes([both[ROWS:] for both in shifted]), axis=1).astype(BF16)
    total = dot(sums, fold_ref[...])
    last = jnp.where(iota((ROWS, 128), 1) < 64, tiles[4], total[:, :128])
    for t, tile in enumerate([*tiles[:4], last, total[:, 128:]]):
        out_ref[:, 128 * t : 128 * (t + 1)] = tile.astype(BF16)


def momentum_kernel(weight_ref, v_ref, out_ref):
    same = (iota((ROWS, ROWS), 0) & 15) == (iota((ROWS, ROWS), 1) & 15)
    acc = jnp.zeros((ROWS, NX), F32)
    for m in range(5):
        window = v_ref[:, 128 * m : 128 * m + WIN]
        move = one(iota((WIN, NX), 0) == iota((WIN, NX), 1) + 16 * m)
        pieces = dot(window, move).astype(BF16)
        if m == 4:
            acc += dot(jnp.where(same, 1.0 / 16, 0.0).astype(BF16), pieces)
        else:
            acc += dot(weight_ref[2 * m], pieces) + dot(weight_ref[2 * m + 1], pieces)
    out_ref[...] = acc.astype(BF16)


VMEM = pl.BlockSpec(memory_space=pltpu.VMEM)
SMEM = pl.BlockSpec(memory_space=pltpu.SMEM)
HBM = pl.BlockSpec(memory_space=pltpu.HBM)


def call(kernel, outs, specs, scratch=()):
    shapes = [jax.ShapeDtypeStruct(out, BF16) for out in outs]
    return pl.pallas_call(
        kernel,
        out_shape=shapes if len(outs) > 1 else shapes[0],
        in_specs=specs,
        out_specs=[VMEM] * len(outs) if len(outs) > 1 else VMEM,
        scratch_shapes=scratch,
        compiler_params=pltpu.CompilerParams(vmem_limit_bytes=48 << 20),
    )


def blocks_of(neighbours, retarded, injection):
    scratch = [
        pltpu.VMEM((4, ATOMS), I32),
        pltpu.VMEM((NO, 2, ORD), BF16),
        pltpu.VMEM((2, ORD, ORD), BF16),
        pltpu.VMEM((2, ORD, 2 * ORD), BF16),
        pltpu.VMEM((3, ORD, NX), BF16),
        pltpu.SemaphoreType.DMA((6,)),
    ]
    f = call(blocks_kernel, [(ATOMS, 4, 3 * NX)], [HBM, HBM, HBM], scratch)
    operands = (neighbours.T, jnp.swapaxes(injection, 0, 1), retarded)
    return f(*(pltpu.with_memory_space_constraint(x, pltpu.HBM) for x in operands))


def prepared(bond_count, bond_mode, mode_shift, occupation, coupling):
    outs = [(4 * NX, WIN), (8, ROWS, ROWS), (ROWS, ROWS), (4, WIN, NX), (4, 2 * ROWS, ROWS), (640, WIN)]
    f = call(prepare_kernel, outs, [SMEM, SMEM, SMEM, SMEM, VMEM])
    return f(bond_count, bond_mode, mode_shift, occupation.T, coupling)


def image_of(kron, turn, move, step, fold, pieces):
    return call(image_kernel, [(ROWS, ORD)], [VMEM] * 6)(kron, turn, move, step, fold, pieces)


def convolved(weights, pieces):
    return call(momentum_kernel, [(ROWS, NX)], [VMEM, VMEM])(weights, pieces)


def exchange(x, axis):
    return lax.all_to_all(x, axis, split_axis=0, concat_axis=0, tiled=True)


def per_device(retarded, injection, neighbours, bond_count, bond_mode, mode_shift, occupation, coupling):
    sent = blocks_of(neighbours, retarded[0, 0], injection[0, 0])
    kron, weights, *selectors = prepared(bond_count, bond_mode, mode_shift, occupation, coupling[0])
    pieces = exchange(sent, "en")
    imaged = image_of(kron, *selectors, pieces)
    spread = exchange(imaged.reshape(16, 16, ORD), "mom")
    scattered = convolved(weights, spread.reshape(ROWS, ORD))
    back = exchange(scattered.reshape(16, 16, NX), "mom")
    return back.reshape(1, 1, ATOMS, 4, NX).astype(F32)


def solution(mesh):
    en = P("en")
    in_specs = (
        P("mom", "en", None, None, None),
        P("mom", "en", None, None, None),
        P(),
        en,
        P("en", None),
        P(),
        P(),
        P("en", None, None, None),
    )
    return jax.shard_map(
        per_device,
        mesh=mesh,
        in_specs=in_specs,
        out_specs=P("mom", "en", None, None, None),
        check_vma=False,
    )
```

```python
import functools

import jax
import jax.numpy as jnp
from jax import lax
from jax.experimental import pallas as pl
from jax.experimental.pallas import tpu as pltpu
from jax.sharding import PartitionSpec as P

F32, BF16, I32 = jnp.float32, jnp.bfloat16, jnp.int32
NO, NX, ATOMS, ROWS, ORD = 12, 144, 64, 256, 768
HALF, SUB, WIN = 384, 192, 256


def iota(shape, dim):
    return lax.broadcasted_iota(I32, shape, dim)


def one(mask):
    return jnp.where(mask, 1.0, 0.0).astype(BF16)


def dot(a, b):
    return lax.dot_general(a, b, (((1,), (0,)), ((), ())), preferred_element_type=F32)


def dot_t(a, b):
    return lax.dot_general(a, b, (((1,), (1,)), ((), ())), preferred_element_type=F32)


def atom_of(index):
    return (index * 5462) >> 16


def orbital_of(index):
    return index - NO * atom_of(index)


def blocks_kernel(nb_hbm, s_hbm, g_hbm, out_ref, nb_ref, s_ref, g_ref, left_ref, z_ref, sems):
    small = [pltpu.make_async_copy(s_hbm, s_ref, sems.at[4]), pltpu.make_async_copy(nb_hbm, nb_ref, sems.at[5])]
    copies = []
    for t in range(2):
        for part in range(2):
            rows = pl.ds(HALF * t, HALF)
            copies.append(
                pltpu.make_async_copy(g_hbm.at[part, rows, :], g_ref.at[part, rows, :], sems.at[2 * t + part])
            )
    for copy in small + copies:
        copy.start()
    for copy in small:
        copy.wait()
    s_r = s_ref[:, 0, :].astype(F32)
    s_i = s_ref[:, 1, :].astype(F32)
    tall, thin = iota((128, 128), 0), iota((128, NO), 0)
    wide, slot = iota((1, 128), 1), iota((1, NO), 1)
    factors = []
    for t in range(6):
        cols = slice(128 * t, 128 * (t + 1))
        upper = jnp.concatenate([s_r[:, cols], s_i[:, cols]], axis=1).astype(BF16)
        lower = jnp.concatenate([-s_i[:, cols], s_r[:, cols]], axis=1).astype(BF16)
        mine = atom_of(wide + (128 * t + 240))
        for kind in range(2):
            if kind:
                near = tall + jnp.where(tall < 64, 128 * (t + 1) + 240, 128 * (t - 1) + 240)
                pick = thin + jnp.where(thin < 64, 128 * (t + 1) + 240, 128 * (t - 1) + 240)
            else:
                near, pick = tall + (128 * t + 240), thin + (128 * t + 240)
            spread = one(orbital_of(pick) == slot)
            same = atom_of(near) == mine
            same = jnp.concatenate([same, same], axis=1)
            halves = [jnp.where(same, dot(spread, x), 0.0).astype(BF16) for x in (upper, lower)]
            factors.append(jnp.concatenate(halves, axis=0))
    lane = iota((HALF, 128), 1)
    for half in range(2):
        rows = slice(HALF * half, HALF * (half + 1))
        copies[2 * half].wait()
        copies[2 * half + 1].wait()
        tiles = [[g_ref[part, rows, 128 * t : 128 * (t + 1)] for part in range(2)] for t in range(6)]
        for t in range(6):
            low, high = tiles[max(t - 1, 0)], tiles[min(t + 1, 5)]
            beside = [jnp.where(lane < 64, high[part], low[part]) for part in range(2)]
            line = dot(jnp.concatenate(tiles[t], axis=1), factors[2 * t])
            line += dot(jnp.concatenate(beside, axis=1), factors[2 * t + 1])
            line = line.astype(BF16)
            left_ref[0, rows, 256 * t : 256 * t + 256] = line
            left_ref[1, rows, 256 * t : 256 * t + 128] = line[:, 128:]
            left_ref[1, rows, 256 * t + 128 : 256 * t + 256] = -line[:, :128]
    own = atom_of(iota((1, NX), 1)) == orbital_of(iota((SUB, NX), 0))

    def products(half, odd):
        mine = slice(HALF * half + SUB * odd, HALF * half + SUB * (odd + 1))
        window = slice(HALF * half + 128 * odd, HALF * half + 128 * odd + WIN)
        stacked = jnp.concatenate([left_ref[0, mine, :], left_ref[1, mine, :]], axis=0)
        cols = [slice(128 * t, 128 * (t + 1)) for t in range(6)]
        right = jnp.concatenate([g_ref[part, window, col] for col in cols for part in range(2)], axis=1)
        return dot_t(stacked, right)

    def finish(half, odd, lesser):
        base = HALF * half
        square = slice(base + 128 * odd, base + 128 * odd + WIN)
        inner = slice(64 * odd, 64 * odd + SUB)
        shift = []
        for part, sign in ((0, -1.0), (1, 1.0)):
            plain = g_ref[part, square, square].astype(F32)
            shift.append(plain[inner] + sign * plain.T[inner])
        row, col = iota((SUB, WIN), 0) + SUB * odd, iota((1, WIN), 1) + 128 * odd
        diagonal = atom_of(row) == atom_of(col)
        fold = one(orbital_of(iota((WIN, NX), 0) + 128 * odd) == orbital_of(iota((1, NX), 1)))
        values = [lesser[:SUB], lesser[SUB:], jnp.where(row > col, shift[0], shift[1])]
        for c, value in enumerate(values):
            folded = dot(jnp.where(diagonal, value, 0.0).astype(BF16), fold)
            z_ref[c, base + SUB * odd : base + SUB * (odd + 1), :] = jnp.where(own, folded, 0.0).astype(BF16)

    todo = [(0, 0), (0, 1), (1, 0), (1, 1)]
    ahead = products(*todo[0])
    for w in range(4):
        lesser = ahead
        if w < 3:
            ahead = products(*todo[w + 1])
        finish(*todo[w], lesser)
    gather = one(atom_of(iota((ATOMS, ORD), 1)) == iota((ATOMS, ORD), 0))
    blocks = jnp.concatenate([dot(gather, z_ref[c]) for c in range(3)], axis=1).astype(BF16)
    owner = one(iota((ROWS, ATOMS), 0) >> 2 == iota((ROWS, ATOMS), 1))
    atoms = dot_t(owner, nb_ref[...].astype(F32).astype(BF16)).astype(I32)
    bond = iota((ROWS, 1), 0) & 3
    wanted = atoms[:, 0:1]
    for m in range(1, 4):
        wanted = jnp.where(bond == m, atoms[:, m : m + 1], wanted)
    sent = dot(one(iota((ROWS, ATOMS), 1) == wanted), blocks)
    out_ref[...] = sent.reshape(ATOMS, 4, 3 * NX).astype(BF16)


def prepare_kernel(
    count_ref,
    mode_ref,
    shift_ref,
    n_ref,
    c_ref,
    kron_ref,
    turn_ref,
    part_ref,
    pair_ref,
    single_ref,
    weight_ref,
    move_ref,
    unpack_ref,
):
    lane = iota((1, WIN), 1)
    entry = jnp.where(lane < 128, lane, 128 + (lane & 15))
    factors = []
    for outer in (True, False):
        wide = (atom_of if outer else orbital_of)(entry)
        spread = jnp.where(iota((NO, WIN), 0) == wide, 1.0, 0.0)
        stacked = lax.dot_general(
            jnp.concatenate([c_ref[m].T for m in range(4)], axis=0),
            spread,
            (((1,), (0,)), ((), ())),
            precision=lax.Precision.HIGHEST,
            preferred_element_type=F32,
        )
        high = stacked.astype(BF16)
        rest = stacked - high.astype(F32)
        middle = rest.astype(BF16)
        low = (rest - middle.astype(F32)).astype(BF16)
        row = iota((4 * NX, 3 * 48), 0)
        j = atom_of(row)
        source = j if outer else NO * atom_of(j) + row - NO * j
        column = iota((1, 3 * 48), 1)
        column = orbital_of(column) + NO * (atom_of(column) & 3)
        factors.append(dot(one(column == source), jnp.concatenate([high, middle, low], axis=0)))
    kron_ref[...] = (factors[0] * factors[1]).astype(BF16)
    row, column = iota((ROWS, ROWS), 0), iota((ROWS, ROWS), 1)
    turn_ref[...] = one(column == ((row & 63) << 2) + (row >> 6))
    x = iota((1, WIN), 1)
    swapped = NO * orbital_of(x) + atom_of(x)
    below = orbital_of(x) < atom_of(x)
    lane = iota((WIN, WIN), 0)
    for c in range(2):
        part_ref[c] = one((lane == x + 16 * c) & (x < NX))
    kept = jnp.where((lane - 32 == x) & (x < NX), 1.0, 0.0)
    turned = jnp.where((lane - 32 == swapped) & (x < NX), 1.0, 0.0)
    part_ref[2] = jnp.where(below, kept, jnp.where(x == swapped, 0.0, -turned)).astype(BF16)
    part_ref[3] = jnp.where(below, turned, kept).astype(BF16)
    part = (row >> 6) - (column >> 6)
    gap = (column & 63) - (row & 63)
    alone = jnp.abs(jnp.where(part == 0, gap, 8 * ROWS))
    facing = jnp.where((row & 128) > 0, -gap, gap)
    facing = jnp.where((part == 0) | (part == 2), facing, 8 * ROWS)
    for m in range(4):
        step = jnp.where(m < count_ref[0], shift_ref[mode_ref[0, m]], 4 * ROWS)
        pair_ref[m] = one(alone == step)
        single_ref[m] = one(facing == step)
    lane = iota((16, ROWS), 1)
    transfer = ((iota((16, ROWS), 0) - ((lane & 63) >> 2)) & 15) + ((lane >> 6) << 4)
    weights = jnp.zeros((16, ROWS), F32)
    for m in range(4):
        for q in range(16):
            weights = jnp.where(transfer == 16 * m + q, n_ref[mode_ref[0, m], q] * (1.0 / 16), weights)
    high = weights.astype(BF16)
    low = (weights - high.astype(F32)).astype(BF16)
    spread = one(iota((ATOMS, 16), 0) >> 2 == iota((ATOMS, 16), 1))
    same = (iota((ATOMS, ROWS), 0) & 3) == (iota((ATOMS, ROWS), 1) & 3)
    weight_ref[:ATOMS, :] = jnp.where(same, dot(spread, high), 0.0).astype(BF16)
    weight_ref[ATOMS:, :] = jnp.where(same, dot(spread, low), 0.0).astype(BF16)
    lane, target = iota((WIN, 640), 0), iota((1, 640), 1)
    tile, slot = target >> 7, (target >> 4) & 7
    wanted = jnp.where(tile < 4, 3 * tile + jnp.where(slot == 4, 2, slot & 1), 12 + slot)
    wanted = jnp.where(slot < jnp.where(tile < 4, 5, 4), wanted, -1)
    move_ref[...] = one((lane >> 4 == wanted) & ((lane & 15) == (target & 15)))
    lane, target = iota((WIN, HALF), 0), iota((1, HALF), 1)
    source = jnp.where(lane < 128, lane, jnp.where((lane >= 192) & (lane < 208), lane - 64, -1))
    slot = (target - 288) >> 4
    x = jnp.where(target < 256, target & 127, 128 + (target & 15))
    real = (target < 128) | (slot == 0)
    inside = (target < 256) | (slot == 0) | (slot == 1)
    swapped = NO * orbital_of(x) + atom_of(x)
    below = orbital_of(x) < atom_of(x)
    kept = jnp.where(inside & (source == x), 1.0, 0.0)
    turned = jnp.where(inside & (source == swapped), 1.0, 0.0)
    if_real = jnp.where(below, kept, jnp.where(x == swapped, 0.0, -turned))
    unpack_ref[...] = jnp.where(real, if_real, jnp.where(below, turned, kept)).astype(BF16)


def image_kernel(kron_ref, turn_ref, part_ref, pair_ref, single_ref, p_ref, out_ref):
    pieces = p_ref[...].astype(F32).reshape(ROWS, 3 * NX).astype(BF16)
    pieces = dot(turn_ref[...], pieces).astype(BF16)
    parts = [dot(pieces[:, 128 * c : 128 * c + WIN], part_ref[c]).astype(BF16) for c in range(2)]
    parts += [dot(pieces[:, WIN:], part_ref[c, :176, :]).astype(BF16) for c in (2, 3)]
    windows = []
    for m in range(4):
        bond = jnp.concatenate([value[ATOMS * m : ATOMS * (m + 1), :NX] for value in parts], axis=0)
        windows.append(dot(bond, kron_ref[NX * m : NX * (m + 1), :]).astype(BF16))
    pairs = [dot(pair_ref[m], windows[m]) for m in range(4)]
    totals = [dot(single_ref[m], windows[m]) for m in range(4)]
    total = (totals[0] + totals[1]) + (totals[2] + totals[3])
    lane = iota((1, WIN), 1)
    entry = jnp.where(lane < 128, lane, 128 + (lane & 15))
    below = orbital_of(entry) < atom_of(entry)
    slot = iota((ATOMS, 128), 1) >> 4
    rest = [jnp.zeros((ATOMS, 128), F32)] * 2
    tiles = []
    for p in range(16):
        m, c = divmod(p, 3)
        if p >= 12:
            value = total[ATOMS * (p - 12) : ATOMS * (p - 11)]
        elif c < 2:
            value = pairs[m][ATOMS * c : ATOMS * (c + 1)]
        else:
            value = jnp.where(below, pairs[m][2 * ATOMS : 3 * ATOMS], pairs[m][3 * ATOMS :])
        tiles.append(value[:, :128])
        rest[p // 8] = jnp.where(slot == p % 8, value[:, 128:], rest[p // 8])
    for t, tile in enumerate(tiles + rest):
        out_ref[:, :, 128 * t : 128 * (t + 1)] = tile.reshape(16, 4, 128).astype(BF16)


def momentum_kernel(weight_ref, move_ref, unpack_ref, v_ref, out_ref):
    v = v_ref[...].astype(F32).reshape(ATOMS, 3 * ORD).astype(BF16)
    rest = dot(v[:, 2048:], move_ref[...]).astype(BF16)
    bonds = [jnp.concatenate([v[:, HALF * m : HALF * (m + 1)], rest[:, 128 * m : 128 * (m + 1)]], axis=1) for m in range(4)]
    bonds = jnp.concatenate(bonds, axis=0)
    lesser = jnp.concatenate([bonds[:, :256], bonds[:, :256], bonds[:, 384:]], axis=1)
    greater = dot(bonds[:, 256:], unpack_ref[...]).astype(BF16)
    greater = jnp.concatenate([jnp.zeros((ROWS, 256), BF16), greater], axis=1)
    total = jnp.concatenate([v[:, 1536:2048], rest[:, 512:]], axis=1)
    total = jnp.concatenate([total, jnp.zeros((ROWS - ATOMS, 640), BF16)], axis=0)
    row, lane = iota((2 * ATOMS, ROWS), 0), iota((2 * ATOMS, ROWS), 1)
    mean = ((row & 3) == (lane & 3)) & (lane < ATOMS) & (row < ATOMS)
    mean = jnp.where(mean, 1.0 / 16, 0.0).astype(BF16)
    weights = weight_ref[...]
    both = dot(
        jnp.concatenate([weights, weights, mean], axis=1), jnp.concatenate([lesser, greater, total], axis=0)
    )
    packed = (both[:ATOMS] + both[ATOMS:])[:, : 4 * NX]
    out_ref[...] = packed.reshape(16, 4, 4 * NX).astype(BF16)


def unpack_kernel(x_ref, out_ref):
    x = x_ref[...].astype(F32).reshape(ATOMS, 4 * NX)
    for c in range(4):
        out_ref[:, c, :128] = x[:, 128 * c : 128 * (c + 1)]
        out_ref[:, c, 128:] = x[:, 512 + 16 * c : 528 + 16 * c]


VMEM = pl.BlockSpec(memory_space=pltpu.VMEM)
SMEM = pl.BlockSpec(memory_space=pltpu.SMEM)
HBM = pl.BlockSpec(memory_space=pltpu.HBM)


def call(kernel, outs, specs, scratch=(), kind=BF16, limit=12):
    shapes = [jax.ShapeDtypeStruct(out, kind) for out in outs]
    return pl.pallas_call(
        kernel,
        out_shape=shapes if len(outs) > 1 else shapes[0],
        in_specs=specs,
        out_specs=[VMEM] * len(outs) if len(outs) > 1 else VMEM,
        scratch_shapes=scratch,
        compiler_params=pltpu.CompilerParams(vmem_limit_bytes=limit << 20),
    )


def blocks_of(neighbours, retarded, injection):
    scratch = [
        pltpu.VMEM((4, ATOMS), I32),
        pltpu.VMEM((NO, 2, ORD), BF16),
        pltpu.VMEM((2, ORD, ORD), BF16),
        pltpu.VMEM((2, ORD, 2 * ORD), BF16),
        pltpu.VMEM((3, ORD, NX), BF16),
        pltpu.SemaphoreType.DMA((6,)),
    ]
    f = call(blocks_kernel, [(ATOMS, 4, 3 * NX)], [HBM, HBM, HBM], scratch, limit=32)
    operands = (neighbours.T, jnp.swapaxes(injection, 0, 1), retarded)
    return f(*(pltpu.with_memory_space_constraint(x, pltpu.HBM) for x in operands))


def prepared(bond_count, bond_mode, mode_shift, occupation, coupling):
    square = (4, ROWS, ROWS)
    for_image = [(4 * NX, WIN), (ROWS, ROWS), square, square, square]
    for_sum = [(2 * ATOMS, ROWS), (WIN, 640), (WIN, HALF)]
    f = call(prepare_kernel, for_image + for_sum, [SMEM, SMEM, SMEM, SMEM, VMEM])
    outs = f(bond_count, bond_mode, mode_shift, occupation.T, coupling)
    return outs[:5], outs[5:]


def image_of(selectors, pieces):
    return call(image_kernel, [(16, 4, 3 * ORD)], [VMEM] * 6)(*selectors, pieces)


def convolved(weights, pieces):
    return call(momentum_kernel, [(16, 4, 4 * NX)], [VMEM] * 4)(*weights, pieces)


def exchange(x, axis):
    return lax.all_to_all(x, axis, split_axis=0, concat_axis=0, tiled=True)


def per_device(retarded, injection, neighbours, bond_count, bond_mode, mode_shift, occupation, coupling):
    sent = blocks_of(neighbours, retarded[0, 0], injection[0, 0])
    selectors, weights = prepared(bond_count, bond_mode, mode_shift, occupation, coupling[0])
    pieces = exchange(sent, "en")
    spread = exchange(image_of(selectors, pieces), "mom")
    back = exchange(convolved(weights, spread), "mom")
    out = call(unpack_kernel, [(ATOMS, 4, NX)], [VMEM], kind=F32)(back)
    return out[None, None]


def solution(mesh):
    en = P("en")
    in_specs = (
        P("mom", "en", None, None, None),
        P("mom", "en", None, None, None),
        P(),
        en,
        P("en", None),
        P(),
        P(),
        P("en", None, None, None),
    )
    return jax.shard_map(
        per_device,
        mesh=mesh,
        in_specs=in_specs,
        out_specs=P("mom", "en", None, None, None),
        check_vma=False,
    )
```

```python
import jax
import jax.numpy as jnp
from jax import lax
from jax.experimental import pallas as pl
from jax.experimental.pallas import tpu as pltpu
from jax.sharding import Mesh
from jax.sharding import PartitionSpec as P

F32, BF16, I32 = jnp.float32, jnp.bfloat16, jnp.int32
NO, NX, ATOMS, ROWS, ORD = 12, 144, 64, 256, 768
HALF, SUB, WIN = 384, 192, 256


def iota(shape, dim):
    return lax.broadcasted_iota(I32, shape, dim)


def one(mask):
    return jnp.where(mask, 1.0, 0.0).astype(BF16)


def dot(a, b):
    return lax.dot_general(a, b, (((1,), (0,)), ((), ())), preferred_element_type=F32)


def dot_t(a, b):
    return lax.dot_general(a, b, (((1,), (1,)), ((), ())), preferred_element_type=F32)


def atom_of(index):
    return (index * 5462) >> 16


def orbital_of(index):
    return index - NO * atom_of(index)


def en_index(place):
    return (((place >> 1) & 7) << 3) + ((place >> 4) << 1) + (place & 1)


def en_place(index):
    return (((index >> 1) & 3) << 4) + ((index >> 3) << 1) + (index & 1)


def mom_index(place):
    return ((place & 7) << 1) + (place >> 3)


def blocks_kernel(nb_hbm, s_hbm, g_hbm, out_ref, nb_ref, s_ref, g_ref, left_ref, z_ref, mask_ref, pick_ref, sems):
    small = [pltpu.make_async_copy(s_hbm, s_ref, sems.at[4]), pltpu.make_async_copy(nb_hbm, nb_ref, sems.at[5])]
    copies = []
    for t in range(2):
        for part in range(2):
            rows = pl.ds(HALF * t, HALF)
            copies.append(
                pltpu.make_async_copy(g_hbm.at[part, rows, :], g_ref.at[part, rows, :], sems.at[2 * t + part])
            )
    for copy in small + copies:
        copy.start()
    tall, thin = iota((128, 128), 0), iota((128, NO), 0)
    wide, slot = iota((1, 128), 1), iota((1, NO), 1)
    for t in range(6):
        mine = atom_of(wide + (128 * t + 240))
        for kind in range(2):
            if kind:
                near = tall + jnp.where(tall < 64, 128 * (t + 1) + 240, 128 * (t - 1) + 240)
                pick = thin + jnp.where(thin < 64, 128 * (t + 1) + 240, 128 * (t - 1) + 240)
            else:
                near, pick = tall + (128 * t + 240), thin + (128 * t + 240)
            mask_ref[2 * t + kind] = one(atom_of(near) == mine)
            pick_ref[2 * t + kind] = one(orbital_of(pick) == slot)
    for copy in small:
        copy.wait()
    s_r = s_ref[:, 0, :].astype(F32)
    s_i = s_ref[:, 1, :].astype(F32)
    factors = []
    for t in range(6):
        cols = slice(128 * t, 128 * (t + 1))
        upper = jnp.concatenate([s_r[:, cols], s_i[:, cols]], axis=1).astype(BF16)
        lower = jnp.concatenate([-s_i[:, cols], s_r[:, cols]], axis=1).astype(BF16)
        for kind in range(2):
            mask = mask_ref[2 * t + kind]
            mask = jnp.concatenate([mask, mask], axis=1)
            halves = [dot(pick_ref[2 * t + kind], x).astype(BF16) * mask for x in (upper, lower)]
            factors.append(jnp.concatenate(halves, axis=0))
    lane = iota((HALF, 128), 1)
    for half in range(2):
        rows = slice(HALF * half, HALF * (half + 1))
        copies[2 * half].wait()
        copies[2 * half + 1].wait()
        tiles = [[g_ref[part, rows, 128 * t : 128 * (t + 1)] for part in range(2)] for t in range(6)]
        for t in range(6):
            low, high = tiles[max(t - 1, 0)], tiles[min(t + 1, 5)]
            beside = [jnp.where(lane < 64, high[part], low[part]) for part in range(2)]
            line = dot(jnp.concatenate(tiles[t], axis=1), factors[2 * t])
            line += dot(jnp.concatenate(beside, axis=1), factors[2 * t + 1])
            line = line.astype(BF16)
            left_ref[0, rows, 256 * t : 256 * t + 256] = line
            left_ref[1, rows, 256 * t : 256 * t + 128] = line[:, 128:]
            left_ref[1, rows, 256 * t + 128 : 256 * t + 256] = -line[:, :128]
    own = atom_of(iota((1, NX), 1)) == orbital_of(iota((SUB, NX), 0))

    def products(half, odd):
        mine = slice(HALF * half + SUB * odd, HALF * half + SUB * (odd + 1))
        window = slice(HALF * half + 128 * odd, HALF * half + 128 * odd + WIN)
        stacked = jnp.concatenate([left_ref[0, mine, :], left_ref[1, mine, :]], axis=0)
        cols = [slice(128 * t, 128 * (t + 1)) for t in range(6)]
        right = jnp.concatenate([g_ref[part, window, col] for col in cols for part in range(2)], axis=1)
        return dot_t(stacked, right)

    def finish(half, odd, lesser):
        base = HALF * half
        square = slice(base + 128 * odd, base + 128 * odd + WIN)
        inner = slice(64 * odd, 64 * odd + SUB)
        shift = []
        for part, sign in ((0, -1.0), (1, 1.0)):
            plain = g_ref[part, square, square].astype(F32)
            shift.append(plain[inner] + sign * plain.T[inner])
        row, col = iota((SUB, WIN), 0) + SUB * odd, iota((1, WIN), 1) + 128 * odd
        diagonal = atom_of(row) == atom_of(col)
        fold = one(orbital_of(iota((WIN, NX), 0) + 128 * odd) == orbital_of(iota((1, NX), 1)))
        values = [lesser[:SUB], lesser[SUB:], jnp.where(row > col, shift[0], shift[1])]
        for c, value in enumerate(values):
            folded = dot(jnp.where(diagonal, value, 0.0).astype(BF16), fold)
            z_ref[c, base + SUB * odd : base + SUB * (odd + 1), :] = jnp.where(own, folded, 0.0).astype(BF16)

    todo = [(0, 0), (0, 1), (1, 0), (1, 1)]
    ahead = products(*todo[0])
    for w in range(4):
        lesser = ahead
        if w < 3:
            ahead = products(*todo[w + 1])
        finish(*todo[w], lesser)
    gather = one(atom_of(iota((ATOMS, ORD), 1)) == iota((ATOMS, ORD), 0))
    blocks = jnp.concatenate([dot(gather, z_ref[c]) for c in range(3)], axis=1).astype(BF16)
    owner = one(en_index(iota((ROWS, ATOMS), 0) >> 2) == iota((ROWS, ATOMS), 1))
    atoms = dot_t(owner, nb_ref[...].astype(F32).astype(BF16)).astype(I32)
    bond = iota((ROWS, 1), 0) & 3
    wanted = atoms[:, 0:1]
    for m in range(1, 4):
        wanted = jnp.where(bond == m, atoms[:, m : m + 1], wanted)
    sent = dot(one(iota((ROWS, ATOMS), 1) == wanted), blocks)
    out_ref[...] = sent.reshape(ATOMS, 4, 3 * NX).astype(BF16)


def prepare_kernel(
    count_ref,
    mode_ref,
    shift_ref,
    n_ref,
    c_ref,
    kron_ref,
    turn_ref,
    part_ref,
    pair_ref,
    single_ref,
    weight_ref,
    move_ref,
    unpack_ref,
):
    lane = iota((1, WIN), 1)
    entry = jnp.where(lane < 128, lane, 128 + (lane & 15))
    factors = []
    for outer in (True, False):
        wide = (atom_of if outer else orbital_of)(entry)
        spread = jnp.where(iota((NO, WIN), 0) == wide, 1.0, 0.0)
        stacked = lax.dot_general(
            jnp.concatenate([c_ref[m].T for m in range(4)], axis=0),
            spread,
            (((1,), (0,)), ((), ())),
            precision=lax.Precision.HIGHEST,
            preferred_element_type=F32,
        )
        high = stacked.astype(BF16)
        rest = stacked - high.astype(F32)
        middle = rest.astype(BF16)
        low = (rest - middle.astype(F32)).astype(BF16)
        row = iota((4 * NX, 3 * 48), 0)
        j = atom_of(row)
        source = j if outer else NO * atom_of(j) + row - NO * j
        column = iota((1, 3 * 48), 1)
        column = orbital_of(column) + NO * (atom_of(column) & 3)
        factors.append(dot(one(column == source), jnp.concatenate([high, middle, low], axis=0)))
    kron_ref[...] = (factors[0] * factors[1]).astype(BF16)
    row, column = iota((ROWS, ROWS), 0), iota((ROWS, ROWS), 1)
    turn_ref[...] = one(column == (en_place(row & 63) << 2) + (row >> 6))
    x = iota((1, WIN), 1)
    swapped = NO * orbital_of(x) + atom_of(x)
    below = orbital_of(x) < atom_of(x)
    lane = iota((WIN, WIN), 0)
    for c in range(2):
        part_ref[c] = one((lane == x + 16 * c) & (x < NX))
    kept = jnp.where((lane - 32 == x) & (x < NX), 1.0, 0.0)
    turned = jnp.where((lane - 32 == swapped) & (x < NX), 1.0, 0.0)
    part_ref[2] = jnp.where(below, kept, jnp.where(x == swapped, 0.0, -turned)).astype(BF16)
    part_ref[3] = jnp.where(below, turned, kept).astype(BF16)
    part = (row >> 6) - (column >> 6)
    gap = (column & 63) - (row & 63)
    alone = jnp.abs(jnp.where(part == 0, gap, 8 * ROWS))
    facing = jnp.where((row & 128) > 0, -gap, gap)
    facing = jnp.where((part == 0) | (part == 2), facing, 8 * ROWS)
    for m in range(4):
        step = jnp.where(m < count_ref[0], shift_ref[mode_ref[0, m]], 4 * ROWS)
        pair_ref[m] = one(alone == step)
        single_ref[m] = one(facing == step)
    lane = iota((16, ROWS), 1)
    transfer = mom_index(iota((16, ROWS), 0)) - mom_index((lane & 63) >> 2)
    transfer = (transfer & 15) + ((lane >> 6) << 4)
    weights = jnp.zeros((16, ROWS), F32)
    for m in range(4):
        for q in range(16):
            weights = jnp.where(transfer == 16 * m + q, n_ref[mode_ref[0, m], q] * (1.0 / 16), weights)
    high = weights.astype(BF16)
    low = (weights - high.astype(F32)).astype(BF16)
    spread = one(iota((ATOMS, 16), 0) >> 2 == iota((ATOMS, 16), 1))
    same = (iota((ATOMS, ROWS), 0) & 3) == (iota((ATOMS, ROWS), 1) & 3)
    weight_ref[:ATOMS, :] = jnp.where(same, dot(spread, high), 0.0).astype(BF16)
    weight_ref[ATOMS:, :] = jnp.where(same, dot(spread, low), 0.0).astype(BF16)
    lane, target = iota((WIN, 640), 0), iota((1, 640), 1)
    tile, slot = target >> 7, (target >> 4) & 7
    wanted = jnp.where(tile < 4, 3 * tile + jnp.where(slot == 4, 2, slot & 1), 12 + slot)
    wanted = jnp.where(slot < jnp.where(tile < 4, 5, 4), wanted, -1)
    move_ref[...] = one((lane >> 4 == wanted) & ((lane & 15) == (target & 15)))
    lane, target = iota((WIN, HALF), 0), iota((1, HALF), 1)
    source = jnp.where(lane < 128, lane, jnp.where((lane >= 192) & (lane < 208), lane - 64, -1))
    slot = (target - 288) >> 4
    x = jnp.where(target < 256, target & 127, 128 + (target & 15))
    real = (target < 128) | (slot == 0)
    inside = (target < 256) | (slot == 0) | (slot == 1)
    swapped = NO * orbital_of(x) + atom_of(x)
    below = orbital_of(x) < atom_of(x)
    kept = jnp.where(inside & (source == x), 1.0, 0.0)
    turned = jnp.where(inside & (source == swapped), 1.0, 0.0)
    if_real = jnp.where(below, kept, jnp.where(x == swapped, 0.0, -turned))
    unpack_ref[...] = jnp.where(real, if_real, jnp.where(below, turned, kept)).astype(BF16)


def image_kernel(kron_ref, turn_ref, part_ref, pair_ref, single_ref, p_ref, out_ref):
    pieces = p_ref[...].astype(F32).reshape(ROWS, 3 * NX).astype(BF16)
    pieces = dot(turn_ref[...], pieces).astype(BF16)
    parts = [dot(pieces[:, 128 * c : 128 * c + WIN], part_ref[c]).astype(BF16) for c in range(2)]
    parts += [dot(pieces[:, WIN:], part_ref[c, :176, :]).astype(BF16) for c in (2, 3)]
    windows = []
    for m in range(4):
        bond = jnp.concatenate([value[ATOMS * m : ATOMS * (m + 1), :NX] for value in parts], axis=0)
        windows.append(dot(bond, kron_ref[NX * m : NX * (m + 1), :]).astype(BF16))
    pairs = [dot(pair_ref[m], windows[m]) for m in range(4)]
    totals = [dot(single_ref[m], windows[m]) for m in range(4)]
    total = (totals[0] + totals[1]) + (totals[2] + totals[3])
    lane = iota((1, WIN), 1)
    entry = jnp.where(lane < 128, lane, 128 + (lane & 15))
    below = orbital_of(entry) < atom_of(entry)
    slot = iota((ATOMS, 128), 1) >> 4
    rest = [jnp.zeros((ATOMS, 128), F32)] * 2
    tiles = []
    for p in range(16):
        m, c = divmod(p, 3)
        if p >= 12:
            value = total[ATOMS * (p - 12) : ATOMS * (p - 11)]
        elif c < 2:
            value = pairs[m][ATOMS * c : ATOMS * (c + 1)]
        else:
            value = jnp.where(below, pairs[m][2 * ATOMS : 3 * ATOMS], pairs[m][3 * ATOMS :])
        tiles.append(value[:, :128])
        rest[p // 8] = jnp.where(slot == p % 8, value[:, 128:], rest[p // 8])
    for t, tile in enumerate(tiles + rest):
        out_ref[:, :, 128 * t : 128 * (t + 1)] = tile.reshape(16, 4, 128).astype(BF16)


def momentum_kernel(weight_ref, move_ref, unpack_ref, v_ref, out_ref):
    v = v_ref[...].astype(F32).reshape(ATOMS, 3 * ORD).astype(BF16)
    rest = dot(v[:, 2048:], move_ref[...]).astype(BF16)
    bonds = [jnp.concatenate([v[:, HALF * m : HALF * (m + 1)], rest[:, 128 * m : 128 * (m + 1)]], axis=1) for m in range(4)]
    bonds = jnp.concatenate(bonds, axis=0)
    lesser = jnp.concatenate([bonds[:, :256], bonds[:, :256], bonds[:, 384:]], axis=1)
    greater = dot(bonds[:, 256:], unpack_ref[...]).astype(BF16)
    greater = jnp.concatenate([jnp.zeros((ROWS, 256), BF16), greater], axis=1)
    total = jnp.concatenate([v[:, 1536:2048], rest[:, 512:]], axis=1)
    total = jnp.concatenate([total, jnp.zeros((ROWS - ATOMS, 640), BF16)], axis=0)
    row, lane = iota((2 * ATOMS, ROWS), 0), iota((2 * ATOMS, ROWS), 1)
    mean = ((row & 3) == (lane & 3)) & (lane < ATOMS) & (row < ATOMS)
    mean = jnp.where(mean, 1.0 / 16, 0.0).astype(BF16)
    weights = weight_ref[...]
    both = dot(
        jnp.concatenate([weights, weights, mean], axis=1), jnp.concatenate([lesser, greater, total], axis=0)
    )
    packed = (both[:ATOMS] + both[ATOMS:])[:, : 4 * NX]
    out_ref[...] = packed.reshape(16, 4, 4 * NX).astype(BF16)


def unpack_kernel(x_ref, out_ref):
    x = x_ref[...].astype(F32).reshape(ATOMS, 4 * NX)
    for c in range(4):
        out_ref[:, c, :128] = x[:, 128 * c : 128 * (c + 1)]
        out_ref[:, c, 128:] = x[:, 512 + 16 * c : 528 + 16 * c]


VMEM = pl.BlockSpec(memory_space=pltpu.VMEM)
SMEM = pl.BlockSpec(memory_space=pltpu.SMEM)
HBM = pl.BlockSpec(memory_space=pltpu.HBM)


def call(kernel, outs, specs, scratch=(), kind=BF16, limit=12):
    shapes = [jax.ShapeDtypeStruct(out, kind) for out in outs]
    return pl.pallas_call(
        kernel,
        out_shape=shapes if len(outs) > 1 else shapes[0],
        in_specs=specs,
        out_specs=[VMEM] * len(outs) if len(outs) > 1 else VMEM,
        scratch_shapes=scratch,
        compiler_params=pltpu.CompilerParams(vmem_limit_bytes=limit << 20),
    )


def blocks_of(neighbours, retarded, injection):
    scratch = [
        pltpu.VMEM((4, ATOMS), I32),
        pltpu.VMEM((NO, 2, ORD), BF16),
        pltpu.VMEM((2, ORD, ORD), BF16),
        pltpu.VMEM((2, ORD, 2 * ORD), BF16),
        pltpu.VMEM((3, ORD, NX), BF16),
        pltpu.VMEM((12, 128, 128), BF16),
        pltpu.VMEM((12, 128, NO), BF16),
        pltpu.SemaphoreType.DMA((6,)),
    ]
    f = call(blocks_kernel, [(ATOMS, 4, 3 * NX)], [HBM, HBM, HBM], scratch, limit=32)
    operands = (neighbours.T, jnp.swapaxes(injection, 0, 1), retarded)
    return f(*(pltpu.with_memory_space_constraint(x, pltpu.HBM) for x in operands))


def prepared(bond_count, bond_mode, mode_shift, occupation, coupling):
    square = (4, ROWS, ROWS)
    for_image = [(4 * NX, WIN), (ROWS, ROWS), square, square, square]
    for_sum = [(2 * ATOMS, ROWS), (WIN, 640), (WIN, HALF)]
    f = call(prepare_kernel, for_image + for_sum, [SMEM, SMEM, SMEM, SMEM, VMEM])
    outs = f(bond_count, bond_mode, mode_shift, occupation.T, coupling)
    return outs[:5], outs[5:]


def image_of(selectors, pieces):
    return call(image_kernel, [(16, 4, 3 * ORD)], [VMEM] * 6)(*selectors, pieces)


def convolved(weights, pieces):
    return call(momentum_kernel, [(16, 4, 4 * NX)], [VMEM] * 4)(*weights, pieces)


def exchange(x, axis):
    return lax.all_to_all(x, axis, split_axis=0, concat_axis=0, tiled=True)


def per_device(retarded, injection, neighbours, bond_count, bond_mode, mode_shift, occupation, coupling):
    sent = blocks_of(neighbours, retarded[0, 0], injection[0, 0])
    selectors, weights = prepared(bond_count, bond_mode, mode_shift, occupation, coupling[0])
    pieces = exchange(sent, ("y_hi", "z", "core"))
    spread = exchange(image_of(selectors, pieces), ("y_lo", "x"))
    back = exchange(convolved(weights, spread), ("y_lo", "x"))
    out = call(unpack_kernel, [(ATOMS, 4, NX)], [VMEM], kind=F32)(back)
    return out[None, None]


def solution(mesh):
    axes = ("x", "y_lo", "z", "y_hi", "core")
    mesh = Mesh(mesh.devices.reshape(8, 2, 8, 4, 2), axes)
    mom, en = axes[:2], axes[2:]
    in_specs = (
        P(mom, en, None, None, None),
        P(mom, en, None, None, None),
        P(),
        P(en),
        P(en, None),
        P(),
        P(),
        P(en, None, None, None),
    )
    return jax.shard_map(
        per_device,
        mesh=mesh,
        in_specs=in_specs,
        out_specs=P(mom, en, None, None, None),
        check_vma=False,
    )
```

```python
import jax
import jax.numpy as jnp
from jax import lax
from jax.experimental import pallas as pl
from jax.experimental.pallas import tpu as pltpu
from jax.sharding import Mesh
from jax.sharding import PartitionSpec as P

F32, BF16, I32 = jnp.float32, jnp.bfloat16, jnp.int32
NO, NX, ATOMS, ROWS, ORD = 12, 144, 64, 256, 768
HALF, SUB, WIN = 384, 192, 256


def iota(shape, dim):
    return lax.broadcasted_iota(I32, shape, dim)


def one(mask):
    return jnp.where(mask, 1.0, 0.0).astype(BF16)


def dot(a, b):
    return lax.dot_general(a, b, (((1,), (0,)), ((), ())), preferred_element_type=F32)


def dot_t(a, b):
    return lax.dot_general(a, b, (((1,), (1,)), ((), ())), preferred_element_type=F32)


def atom_of(index):
    return (index * 5462) >> 16


def orbital_of(index):
    return index - NO * atom_of(index)


def en_index(place):
    return (((place >> 1) & 7) << 3) + ((place >> 4) << 1) + (place & 1)


def en_place(index):
    return (((index >> 1) & 3) << 4) + ((index >> 3) << 1) + (index & 1)


def mom_index(place):
    return ((place & 7) << 1) + (place >> 3)


def energy_of(row):
    return (mom_index(row >> 2) << 2) + (row & 3)


def blocks_kernel(nb_hbm, s_hbm, g_hbm, out_ref, nb_ref, s_ref, g_ref, left_ref, z_ref, mask_ref, pick_ref, sems):
    small = [pltpu.make_async_copy(s_hbm, s_ref, sems.at[4]), pltpu.make_async_copy(nb_hbm, nb_ref, sems.at[5])]
    copies = []
    for t in range(2):
        for part in range(2):
            rows = pl.ds(HALF * t, HALF)
            copies.append(
                pltpu.make_async_copy(g_hbm.at[part, rows, :], g_ref.at[part, rows, :], sems.at[2 * t + part])
            )
    for copy in small + copies:
        copy.start()
    tall, thin = iota((128, 128), 0), iota((128, NO), 0)
    wide, slot = iota((1, 128), 1), iota((1, NO), 1)
    for t in range(6):
        mine = atom_of(wide + (128 * t + 240))
        for kind in range(2):
            if kind:
                near = tall + jnp.where(tall < 64, 128 * (t + 1) + 240, 128 * (t - 1) + 240)
                pick = thin + jnp.where(thin < 64, 128 * (t + 1) + 240, 128 * (t - 1) + 240)
            else:
                near, pick = tall + (128 * t + 240), thin + (128 * t + 240)
            mask_ref[2 * t + kind] = one(atom_of(near) == mine)
            pick_ref[2 * t + kind] = one(orbital_of(pick) == slot)
    for copy in small:
        copy.wait()
    s_r = s_ref[:, 0, :].astype(F32)
    s_i = s_ref[:, 1, :].astype(F32)
    factors = []
    for t in range(6):
        cols = slice(128 * t, 128 * (t + 1))
        upper = jnp.concatenate([s_r[:, cols], s_i[:, cols]], axis=1).astype(BF16)
        lower = jnp.concatenate([-s_i[:, cols], s_r[:, cols]], axis=1).astype(BF16)
        for kind in range(2):
            mask = mask_ref[2 * t + kind]
            mask = jnp.concatenate([mask, mask], axis=1)
            halves = [dot(pick_ref[2 * t + kind], x).astype(BF16) * mask for x in (upper, lower)]
            factors.append(jnp.concatenate(halves, axis=0))
    lane = iota((HALF, 128), 1)
    for half in range(2):
        rows = slice(HALF * half, HALF * (half + 1))
        copies[2 * half].wait()
        copies[2 * half + 1].wait()
        tiles = [[g_ref[part, rows, 128 * t : 128 * (t + 1)] for part in range(2)] for t in range(6)]
        for t in range(6):
            low, high = tiles[max(t - 1, 0)], tiles[min(t + 1, 5)]
            beside = [jnp.where(lane < 64, high[part], low[part]) for part in range(2)]
            line = dot(jnp.concatenate(tiles[t], axis=1), factors[2 * t])
            line += dot(jnp.concatenate(beside, axis=1), factors[2 * t + 1])
            line = line.astype(BF16)
            left_ref[0, rows, 256 * t : 256 * t + 256] = line
            left_ref[1, rows, 256 * t : 256 * t + 128] = line[:, 128:]
            left_ref[1, rows, 256 * t + 128 : 256 * t + 256] = -line[:, :128]
    own = atom_of(iota((1, NX), 1)) == orbital_of(iota((SUB, NX), 0))

    def products(half, odd):
        mine = slice(HALF * half + SUB * odd, HALF * half + SUB * (odd + 1))
        window = slice(HALF * half + 128 * odd, HALF * half + 128 * odd + WIN)
        stacked = jnp.concatenate([left_ref[0, mine, :], left_ref[1, mine, :]], axis=0)
        cols = [slice(128 * t, 128 * (t + 1)) for t in range(6)]
        right = jnp.concatenate([g_ref[part, window, col] for col in cols for part in range(2)], axis=1)
        return dot_t(stacked, right)

    def finish(half, odd, lesser):
        base = HALF * half
        square = slice(base + 128 * odd, base + 128 * odd + WIN)
        inner = slice(64 * odd, 64 * odd + SUB)
        shift = []
        for part, sign in ((0, -1.0), (1, 1.0)):
            plain = g_ref[part, square, square].astype(F32)
            shift.append(plain[inner] + sign * plain.T[inner])
        row, col = iota((SUB, WIN), 0) + SUB * odd, iota((1, WIN), 1) + 128 * odd
        diagonal = atom_of(row) == atom_of(col)
        fold = one(orbital_of(iota((WIN, NX), 0) + 128 * odd) == orbital_of(iota((1, NX), 1)))
        values = [lesser[:SUB], lesser[SUB:], jnp.where(row > col, shift[0], shift[1])]
        for c, value in enumerate(values):
            folded = dot(jnp.where(diagonal, value, 0.0).astype(BF16), fold)
            z_ref[c, base + SUB * odd : base + SUB * (odd + 1), :] = jnp.where(own, folded, 0.0).astype(BF16)

    todo = [(0, 0), (0, 1), (1, 0), (1, 1)]
    ahead = products(*todo[0])
    for w in range(4):
        lesser = ahead
        if w < 3:
            ahead = products(*todo[w + 1])
        finish(*todo[w], lesser)
    gather = one(atom_of(iota((ATOMS, ORD), 1)) == iota((ATOMS, ORD), 0))
    blocks = jnp.concatenate([dot(gather, z_ref[c]) for c in range(3)], axis=1).astype(BF16)
    owner = one(en_index(iota((ROWS, ATOMS), 0) >> 2) == iota((ROWS, ATOMS), 1))
    atoms = dot_t(owner, nb_ref[...].astype(F32).astype(BF16)).astype(I32)
    bond = iota((ROWS, 1), 0) & 3
    wanted = atoms[:, 0:1]
    for m in range(1, 4):
        wanted = jnp.where(bond == m, atoms[:, m : m + 1], wanted)
    sent = dot(one(iota((ROWS, ATOMS), 1) == wanted), blocks)
    out_ref[...] = sent.reshape(ATOMS, 4, 3 * NX).astype(BF16)


def prepare_kernel(
    count_ref,
    mode_ref,
    shift_ref,
    n_ref,
    c_ref,
    kron_ref,
    turn_ref,
    part_ref,
    pair_ref,
    single_ref,
    weight_ref,
    move_ref,
    unpack_ref,
):
    lane = iota((1, WIN), 1)
    entry = jnp.where(lane < 128, lane, 128 + (lane & 15))
    factors = []
    for outer in (True, False):
        wide = (atom_of if outer else orbital_of)(entry)
        spread = jnp.where(iota((NO, WIN), 0) == wide, 1.0, 0.0)
        stacked = lax.dot_general(
            jnp.concatenate([c_ref[m].T for m in range(4)], axis=0),
            spread,
            (((1,), (0,)), ((), ())),
            precision=lax.Precision.HIGHEST,
            preferred_element_type=F32,
        )
        high = stacked.astype(BF16)
        rest = stacked - high.astype(F32)
        middle = rest.astype(BF16)
        low = (rest - middle.astype(F32)).astype(BF16)
        row = iota((4 * NX, 3 * 48), 0)
        j = atom_of(row)
        source = j if outer else NO * atom_of(j) + row - NO * j
        column = iota((1, 3 * 48), 1)
        column = orbital_of(column) + NO * (atom_of(column) & 3)
        factors.append(dot(one(column == source), jnp.concatenate([high, middle, low], axis=0)))
    kron_ref[...] = (factors[0] * factors[1]).astype(BF16)
    row, column = iota((ROWS, ROWS), 0), iota((ROWS, ROWS), 1)
    turn_ref[...] = one(column == (en_place(energy_of(row & 63)) << 2) + (row >> 6))
    x = iota((1, WIN), 1)
    swapped = NO * orbital_of(x) + atom_of(x)
    below = orbital_of(x) < atom_of(x)
    lane = iota((WIN, WIN), 0)
    for c in range(2):
        part_ref[c] = one((lane == x + 16 * c) & (x < NX))
    kept = jnp.where((lane - 32 == x) & (x < NX), 1.0, 0.0)
    turned = jnp.where((lane - 32 == swapped) & (x < NX), 1.0, 0.0)
    part_ref[2] = jnp.where(below, kept, jnp.where(x == swapped, 0.0, -turned)).astype(BF16)
    part_ref[3] = jnp.where(below, turned, kept).astype(BF16)
    part = (row >> 6) - (column >> 6)
    gap = energy_of(column & 63) - energy_of(row & 63)
    alone = jnp.abs(jnp.where(part == 0, gap, 8 * ROWS))
    facing = jnp.where((row & 128) > 0, -gap, gap)
    facing = jnp.where((part == 0) | (part == 2), facing, 8 * ROWS)
    for m in range(4):
        step = jnp.where(m < count_ref[0], shift_ref[mode_ref[0, m]], 4 * ROWS)
        pair_ref[m] = one(alone == step)
        single_ref[m] = one(facing == step)
    lane = iota((16, ROWS), 1)
    transfer = iota((16, ROWS), 0) - mom_index((lane & 63) >> 2)
    transfer = (transfer & 15) + ((lane >> 6) << 4)
    weights = jnp.zeros((16, ROWS), F32)
    for m in range(4):
        for q in range(16):
            weights = jnp.where(transfer == 16 * m + q, n_ref[mode_ref[0, m], q] * (1.0 / 16), weights)
    high = weights.astype(BF16)
    low = (weights - high.astype(F32)).astype(BF16)
    spread = one(iota((ATOMS, 16), 0) >> 2 == iota((ATOMS, 16), 1))
    same = (iota((ATOMS, ROWS), 0) & 3) == (iota((ATOMS, ROWS), 1) & 3)
    weight_ref[:ATOMS, :] = jnp.where(same, dot(spread, high), 0.0).astype(BF16)
    weight_ref[ATOMS:, :] = jnp.where(same, dot(spread, low), 0.0).astype(BF16)
    lane, target = iota((WIN, 640), 0), iota((1, 640), 1)
    tile, slot = target >> 7, (target >> 4) & 7
    wanted = jnp.where(tile < 4, 3 * tile + jnp.where(slot == 4, 2, slot & 1), 12 + slot)
    wanted = jnp.where(slot < jnp.where(tile < 4, 5, 4), wanted, -1)
    move_ref[...] = one((lane >> 4 == wanted) & ((lane & 15) == (target & 15)))
    lane, target = iota((WIN, HALF), 0), iota((1, HALF), 1)
    source = jnp.where(lane < 128, lane, jnp.where((lane >= 192) & (lane < 208), lane - 64, -1))
    slot = (target - 288) >> 4
    x = jnp.where(target < 256, target & 127, 128 + (target & 15))
    real = (target < 128) | (slot == 0)
    inside = (target < 256) | (slot == 0) | (slot == 1)
    swapped = NO * orbital_of(x) + atom_of(x)
    below = orbital_of(x) < atom_of(x)
    kept = jnp.where(inside & (source == x), 1.0, 0.0)
    turned = jnp.where(inside & (source == swapped), 1.0, 0.0)
    if_real = jnp.where(below, kept, jnp.where(x == swapped, 0.0, -turned))
    unpack_ref[...] = jnp.where(real, if_real, jnp.where(below, turned, kept)).astype(BF16)


def image_kernel(kron_ref, turn_ref, part_ref, pair_ref, single_ref, p_ref, out_ref):
    pieces = p_ref[...].astype(F32).reshape(ROWS, 3 * NX).astype(BF16)
    pieces = dot(turn_ref[...], pieces).astype(BF16)
    parts = [dot(pieces[:, 128 * c : 128 * c + WIN], part_ref[c]).astype(BF16) for c in range(2)]
    parts += [dot(pieces[:, WIN:], part_ref[c, :176, :]).astype(BF16) for c in (2, 3)]
    windows = []
    for m in range(4):
        bond = jnp.concatenate([value[ATOMS * m : ATOMS * (m + 1), :NX] for value in parts], axis=0)
        windows.append(dot(bond, kron_ref[NX * m : NX * (m + 1), :]).astype(BF16))
    pairs = [dot(pair_ref[m], windows[m]) for m in range(4)]
    totals = [dot(single_ref[m], windows[m]) for m in range(4)]
    total = (totals[0] + totals[1]) + (totals[2] + totals[3])
    lane = iota((1, WIN), 1)
    entry = jnp.where(lane < 128, lane, 128 + (lane & 15))
    below = orbital_of(entry) < atom_of(entry)
    slot = iota((ATOMS, 128), 1) >> 4
    rest = [jnp.zeros((ATOMS, 128), F32)] * 2
    tiles = []
    for p in range(16):
        m, c = divmod(p, 3)
        if p >= 12:
            value = total[ATOMS * (p - 12) : ATOMS * (p - 11)]
        elif c < 2:
            value = pairs[m][ATOMS * c : ATOMS * (c + 1)]
        else:
            value = jnp.where(below, pairs[m][2 * ATOMS : 3 * ATOMS], pairs[m][3 * ATOMS :])
        tiles.append(value[:, :128])
        rest[p // 8] = jnp.where(slot == p % 8, value[:, 128:], rest[p // 8])
    for t, tile in enumerate(tiles + rest):
        out_ref[:, :, 128 * t : 128 * (t + 1)] = tile.reshape(16, 4, 128).astype(BF16)


def momentum_kernel(weight_ref, move_ref, unpack_ref, v_ref, out_ref):
    v = v_ref[...].astype(F32).reshape(ATOMS, 3 * ORD).astype(BF16)
    rest = dot(v[:, 2048:], move_ref[...]).astype(BF16)
    bonds = [jnp.concatenate([v[:, HALF * m : HALF * (m + 1)], rest[:, 128 * m : 128 * (m + 1)]], axis=1) for m in range(4)]
    bonds = jnp.concatenate(bonds, axis=0)
    lesser = jnp.concatenate([bonds[:, :256], bonds[:, :256], bonds[:, 384:]], axis=1)
    greater = dot(bonds[:, 256:], unpack_ref[...]).astype(BF16)
    greater = jnp.concatenate([jnp.zeros((ROWS, 256), BF16), greater], axis=1)
    total = jnp.concatenate([v[:, 1536:2048], rest[:, 512:]], axis=1)
    total = jnp.concatenate([total, jnp.zeros((ROWS - ATOMS, 640), BF16)], axis=0)
    row, lane = iota((2 * ATOMS, ROWS), 0), iota((2 * ATOMS, ROWS), 1)
    mean = ((row & 3) == (lane & 3)) & (lane < ATOMS) & (row < ATOMS)
    mean = jnp.where(mean, 1.0 / 16, 0.0).astype(BF16)
    weights = weight_ref[...]
    both = dot(
        jnp.concatenate([weights, weights, mean], axis=1), jnp.concatenate([lesser, greater, total], axis=0)
    )
    packed = (both[:ATOMS] + both[ATOMS:])[:, : 4 * NX]
    out_ref[...] = packed.reshape(16, 4, 4 * NX).astype(BF16)


def unpack_kernel(x_ref, out_ref):
    x = x_ref[...].astype(F32).reshape(ATOMS, 4 * NX)
    for c in range(4):
        out_ref[:, c, :128] = x[:, 128 * c : 128 * (c + 1)]
        out_ref[:, c, 128:] = x[:, 512 + 16 * c : 528 + 16 * c]


VMEM = pl.BlockSpec(memory_space=pltpu.VMEM)
SMEM = pl.BlockSpec(memory_space=pltpu.SMEM)
HBM = pl.BlockSpec(memory_space=pltpu.HBM)


def call(kernel, outs, specs, scratch=(), kind=BF16, limit=12):
    shapes = [jax.ShapeDtypeStruct(out, kind) for out in outs]
    return pl.pallas_call(
        kernel,
        out_shape=shapes if len(outs) > 1 else shapes[0],
        in_specs=specs,
        out_specs=[VMEM] * len(outs) if len(outs) > 1 else VMEM,
        scratch_shapes=scratch,
        compiler_params=pltpu.CompilerParams(vmem_limit_bytes=limit << 20),
    )


def blocks_of(neighbours, retarded, injection):
    scratch = [
        pltpu.VMEM((4, ATOMS), I32),
        pltpu.VMEM((NO, 2, ORD), BF16),
        pltpu.VMEM((2, ORD, ORD), BF16),
        pltpu.VMEM((2, ORD, 2 * ORD), BF16),
        pltpu.VMEM((3, ORD, NX), BF16),
        pltpu.VMEM((12, 128, 128), BF16),
        pltpu.VMEM((12, 128, NO), BF16),
        pltpu.SemaphoreType.DMA((6,)),
    ]
    f = call(blocks_kernel, [(ATOMS, 4, 3 * NX)], [HBM, HBM, HBM], scratch, limit=32)
    operands = (neighbours.T, jnp.swapaxes(injection, 0, 1), retarded)
    return f(*(pltpu.with_memory_space_constraint(x, pltpu.HBM) for x in operands))


def prepared(bond_count, bond_mode, mode_shift, occupation, coupling):
    square = (4, ROWS, ROWS)
    for_image = [(4 * NX, WIN), (ROWS, ROWS), square, square, square]
    for_sum = [(2 * ATOMS, ROWS), (WIN, 640), (WIN, HALF)]
    f = call(prepare_kernel, for_image + for_sum, [SMEM, SMEM, SMEM, SMEM, VMEM])
    outs = f(bond_count, bond_mode, mode_shift, occupation.T, coupling)
    return outs[:5], outs[5:]


def image_of(selectors, pieces):
    return call(image_kernel, [(16, 4, 3 * ORD)], [VMEM] * 6)(*selectors, pieces)


def convolved(weights, pieces):
    return call(momentum_kernel, [(16, 4, 4 * NX)], [VMEM] * 4)(*weights, pieces)


def exchange(x, axis):
    return lax.all_to_all(x, axis, split_axis=0, concat_axis=0, tiled=True)


def per_device(retarded, injection, neighbours, bond_count, bond_mode, mode_shift, occupation, coupling):
    sent = blocks_of(neighbours, retarded[0, 0], injection[0, 0])
    selectors, weights = prepared(bond_count, bond_mode, mode_shift, occupation, coupling[0])
    pieces = exchange(sent, ("y_hi", "z", "core"))
    spread = exchange(image_of(selectors, pieces), ("y_lo", "x"))
    back = exchange(convolved(weights, spread), ("x", "y_lo"))
    out = call(unpack_kernel, [(ATOMS, 4, NX)], [VMEM], kind=F32)(back)
    return out[None, None]


def solution(mesh):
    axes = ("x", "y_lo", "z", "y_hi", "core")
    mesh = Mesh(mesh.devices.reshape(8, 2, 8, 4, 2), axes)
    mom, en = axes[:2], axes[2:]
    in_specs = (
        P(mom, en, None, None, None),
        P(mom, en, None, None, None),
        P(),
        P(en),
        P(en, None),
        P(),
        P(),
        P(en, None, None, None),
    )
    return jax.shard_map(
        per_device,
        mesh=mesh,
        in_specs=in_specs,
        out_specs=P(mom, en, None, None, None),
        check_vma=False,
    )
```
